32 devices in a mesh: samp: 4 (over y, x), var: 8 (over z, core).
Axes of the slice: x: 2, y: 2, z: 4, core: 2. Of those that a mesh axis runs over, the one named last changes fastest.
Arguments:
- observed: bfloat16 [1024, 32768], P('samp', 'var'), may hold values from -6 to 6
- blocks: float32 [256, 2, 128, 128], P('var'), may hold values from -6 to 6
- diagonal: float32 [32768], P('var'), may hold values from 1 to 4
- pattern: int32 [256, 2], P('var'), may hold values from 0 to 255, as said below
Outputs:
- new_blocks: float32 [256, 2, 128, 128], P('var')
- new_diagonal: float32 [32768], P('var')
- objective: float32 [2], replicated
The draws below stay inside these ranges and needn't reach their ends.
Inputs may be any that keep to these rules, and one draw needn't show every extreme that they name: pattern[c, 0] and pattern[c, 1] are two different row-block indices, one of them equal to c. For each index v of var, among its block columns c = v * 32 to v * 32 + 31, for every u, at most 4 of the entries that differ from c name row blocks in the range u * 32 to u * 32 + 31, and for some u exactly 4 do.
All inputs are finite; a program needn't handle non-finite values.
Results may differ from the reference program's by a relative error of at most 0.0049.
Values may be sent and summed in bfloat16 or wider, within the bound.
A program may use at most 128 MiB of HBM per device.

```python
import math
import jax
import jax.numpy as jnp
from jax import lax

BW = 128
CPD = 32
STEPS = 2
NBC = 256
P_SIZE = 32768
SAMPLES = 1024
CAP = 4
N_VAR = 8


def draw_pattern(key, part):
    first_draw = jax.random.randint(jax.random.fold_in(key, 11), (N_VAR,), 0, N_VAR)
    second_draw = jax.random.randint(jax.random.fold_in(key, 12), (N_VAR,), 0, N_VAR)
    reorder_permutation = jax.random.permutation(jax.random.fold_in(key, 13), N_VAR)
    hot_owner = reorder_permutation[first_draw * second_draw // N_VAR]
    offset = jax.random.randint(jax.random.fold_in(key, 14), (N_VAR, 1), 0, N_VAR - 1)
    position = jnp.arange(CPD, dtype=jnp.int32)[None, :]
    spread = (hot_owner[:, None] + 1 + (position - CAP + offset) % (N_VAR - 1)) % N_VAR
    owners = jnp.where(position < CAP, hot_owner[:, None], spread)
    scores = jax.random.randint(jax.random.fold_in(key, 15), (N_VAR, CPD), 0, 1024) * CPD + position
    column_order = jnp.argsort(scores, axis=1)
    owners = jnp.take_along_axis(owners, column_order, axis=1)
    resident_index = jax.random.randint(jax.random.fold_in(key, 16), (N_VAR, CPD), 0, CPD)
    devices = jnp.arange(N_VAR, dtype=jnp.int32)[:, None]
    own_column = devices * CPD + position
    row_block = owners * CPD + resident_index
    row_block = jnp.where(row_block == own_column, owners * CPD + (resident_index + 1) % CPD, row_block)
    slot_flip = jax.random.randint(jax.random.fold_in(key, 17), (N_VAR, CPD), 0, 2)
    paired = jnp.where((slot_flip == 0)[:, :, None], jnp.stack([own_column, row_block], -1), jnp.stack([row_block, own_column], -1))
    return paired.reshape(NBC, 2).astype(jnp.int32)


def levels(own_key, shape, split, smallest, top_value):
    gain, own = 1.0, jax.random.fold_in(own_key, 6)
    for axis_at, blocks in split:
        draws = jnp.exp(jax.random.uniform(jax.random.fold_in(own, axis_at), (blocks,), jnp.float32, smallest / len(split), top_value / len(split)))
        gain = gain * jnp.repeat(draws, shape[axis_at] // blocks).reshape([-1 if axis == axis_at else 1 for axis in range(len(shape))])
    return gain


def bell_draw(stream_key, dims, scale, most, cuts=(), kind=jnp.bfloat16):
    array = scale * jax.random.normal(stream_key, dims, jnp.float32)
    if cuts:
        array = array * levels(stream_key, dims, cuts, -0.22, 0.18)
    return jnp.clip(array, -most, most).astype(kind)


def setup_inputs(seed: int = 0) -> dict:
    seeds = jax.random.split(jax.random.key(seed), 5)
    observed = bell_draw(seeds[0], (SAMPLES, P_SIZE), 1.0, 6.0, ((0, 4), (1, 8)))
    blocks = bell_draw(seeds[1], (NBC, 2, BW, BW), 1.0, 6.0, ((0, 8),), jnp.float32)
    diagonal = jnp.clip(jnp.exp(math.log(4.0) - 1.3862944 * jax.random.uniform(seeds[2], (P_SIZE,), jnp.float32) ** levels(seeds[2], (P_SIZE,), ((0, 8),), -0.2, 0.2)), 1.0, 4.0)
    pattern = draw_pattern(jax.random.fold_in(seeds[4], 71), 0)
    return {"observed": observed, "blocks": blocks, "diagonal": diagonal, "pattern": pattern}


step_length = 0.5
penalty = 0.5

def shrink(moved, level):
    return jnp.sign(moved) * jnp.maximum(jnp.abs(moved) - level, 0.0)

def reference(observed, blocks, diagonal, pattern):
    block_count = blocks.shape[0]
    block_width = blocks.shape[2]
    sample_count = observed.shape[0]
    matrix_order = block_count * block_width
    group_size = math.gcd(block_count, 64)
    group_count = block_count // group_size
    column_tiles = observed.reshape(sample_count, block_count, block_width)
    columns = jnp.arange(block_count, dtype=jnp.int32)
    on_diag = pattern == columns[:, None]
    diag_mask = jnp.eye(block_width, dtype=bool)
    element_mask = on_diag[:, :, None, None] & diag_mask
    stored = jnp.where(element_mask, jnp.float32(0.0), blocks)
    diag_values = diagonal.reshape(block_count, block_width)

    def column_group(inputs):
        pattern_group, block_group, value_group, flag_group = inputs
        picked = jnp.take(column_tiles, pattern_group.reshape(-1), axis=1)
        picked = picked.reshape(sample_count, group_size, 2, block_width).astype(jnp.float32)
        full_blocks = jnp.where(flag_group[:, :, None, None] & diag_mask, value_group[:, None, None, :], block_group)
        rounded = lax.optimization_barrier(full_blocks.astype(jnp.bfloat16)).astype(jnp.float32)
        product = jnp.einsum('sgkb,gkbn->sgn', picked, rounded, precision=lax.Precision.HIGHEST)
        squares = jnp.sum(product * product)
        lower_precision_product = lax.optimization_barrier(product.astype(jnp.bfloat16)).astype(jnp.float32)
        gradient = jnp.einsum('sgkb,sgn->gkbn', picked, lower_precision_product, precision=lax.Precision.HIGHEST)
        return (gradient, squares)
    objectives = []
    for iteration in range(STEPS):
        gradient, squares = lax.map(column_group, (pattern.reshape(group_count, group_size, 2), stored.reshape(group_count, group_size, 2, block_width, block_width), diag_values.reshape(group_count, group_size, block_width), on_diag.reshape(group_count, group_size, 2)))
        gradient = gradient.reshape(block_count, 2, block_width, block_width) / sample_count
        total = -jnp.sum(jnp.log(diag_values)) + jnp.sum(squares) / (2.0 * sample_count) + penalty * jnp.sum(jnp.abs(stored))
        objectives.append(total / matrix_order)
        moved = stored - step_length * gradient
        stored = jnp.where(element_mask, jnp.float32(0.0), shrink(moved, step_length * penalty))
        along = lax.optimization_barrier(jnp.sum(jnp.where(element_mask, gradient, jnp.float32(0.0)), axis=(1, 2)))
        moved_diag = diag_values - step_length * along
        diag_values = 0.5 * (moved_diag + jnp.sqrt(moved_diag * moved_diag + 4.0 * step_length))
    return (stored, diag_values.reshape(-1), jnp.stack(objectives))
```

```python
import functools

import jax
import jax.numpy as jnp
from jax import lax
from jax.experimental import pallas as pl
from jax.experimental.pallas import tpu as pltpu
from jax.sharding import PartitionSpec as P

STEPS = 2


step_length = 0.5
penalty = 0.5
MESH = pl.DeviceIdType.MESH


def shrink(moved, level):
    return moved - jnp.clip(moved, -level, level)


def flip(index, offset, count):
    out, bit = 0, 1
    while bit < count:
        out = out + ((index // bit + offset // bit) % 2) * bit
        bit *= 2
    return out


def inner_chip(v):
    return ((v // 2 + 1) // 2) % 2


def partner(v, b, k, var):
    half = var // 2
    close = half + 2 * inner_chip(v)
    distant = 2 * half + 2 - close
    high, low = k // 2, k % 2
    return (0, 1, 2 + high, close + low, 3 - high, distant + low, distant + 1 - low, close + 1 - low)[b]


def send_rank(i, n, samp, half):
    if isinstance(i, int) and i < half:
        return (n + (i - 2) * (samp // 2)) % samp
    return 2 * n + i % 2 if n < 2 else 2 * (n - 2) + 1 - i % 2


def main_kernel(samp, var, pat_hbm, x_hbm, blk_hbm, dia_hbm,
                fin_ref, tails_ref, obj_ref, tab_ref,
                pat_ref, x, blk, dia_ref, tab, ask, ask_s, far, farz, cc_out, cc_in, cc_own, cc_diag,
                oo_out, oo_in, oc_own, oo_own, oo_diag, oz, acc,
                load, tab_l, ask_ss, ask_rs, ask_l, cc_s, cc_r, z_s, z_r, oo_s, oo_r, out_s, out_r,
                rel_s, rel_r, tail_s, tail_r, oz_s, oz_r):
    s = lax.axis_index("samp")
    v = lax.axis_index("var")
    inner = inner_chip(v)
    rows, width = x.shape[1], x.shape[2]
    half = var // 2
    fold_rows = width // 2
    total_rows = rows * samp
    over_first = (((0,), (0,)), ((), ()))

    cols = x.shape[0]
    bits = cols.bit_length() - 1
    barrier = pltpu.get_barrier_semaphore()
    for i in range(1, var):
        pl.semaphore_signal(barrier, inc=1, device_id={"var": flip(v, i, var)}, device_id_type=MESH)
    for d in range(1, samp):
        pl.semaphore_signal(barrier, inc=1, device_id={"samp": flip(s, d, samp)}, device_id_type=MESH)

    pat_load = pltpu.make_async_copy(pat_hbm, pat_ref, load.at[cols + 1])
    pat_load.start()
    x_loads = [
        pltpu.make_async_copy(x_hbm.at[:, l * width:(l + 1) * width], x.at[l], load.at[l])
        for l in range(cols)
    ]
    for x_load in x_loads:
        x_load.start()
    blk_load = pltpu.make_async_copy(blk_hbm, blk, load.at[cols])
    dia_load = pltpu.make_async_copy(dia_hbm, dia_ref, load.at[cols + 2])

    pat_load.wait()
    first, second = pat_ref[0:1, :], pat_ref[1:2, :]
    ids = lax.broadcasted_iota(jnp.int32, (1, cols), 1)
    lead = first == v * cols + ids
    off_row = jnp.where(lead, second, first)
    owner = lax.shift_right_logical(off_row, bits)
    entry = (off_row & (cols - 1)) + ids * cols + jnp.where(lead, 0, cols * cols)
    below = lax.broadcasted_iota(jnp.int32, (cols, cols), 0)
    across = lax.broadcasted_iota(jnp.int32, (cols, cols), 1)
    wide = jnp.broadcast_to(owner, (cols, cols))
    down = jnp.sum(jnp.where(below == across, wide, 0), axis=1, keepdims=True)
    rank = jnp.sum(jnp.where((down == wide) & (below < across), 1, 0), axis=0, keepdims=True)
    mine = lax.broadcasted_iota(jnp.int32, (var, cols), 0) == owner
    lanes = lax.broadcasted_iota(jnp.int32, (var, width), 1)
    table = jnp.zeros((var, width), jnp.int32)
    for k in range(samp):
        picked = jnp.sum(jnp.where(mine & (rank == k), entry, 0), axis=1, keepdims=True)
        table = jnp.where(lanes == k, picked, table)
    for u in range(var):
        tab_ref[u] = table[u:u + 1, :]
    tab_load = pltpu.make_async_copy(tab_ref, tab, tab_l)
    tab_load.start()

    pl.semaphore_wait(barrier, samp + var - 2)

    def remote(src, dst, send, recv, **where):
        return pltpu.make_async_remote_copy(
            src_ref=src, dst_ref=dst, send_sem=send, recv_sem=recv,
            device_id=where, device_id_type=MESH)

    def ask_copy(i):
        u = flip(v, i, var)
        return remote(tab_ref.at[u], ask.at[v], ask_ss.at[i], ask_rs.at[i], var=u)

    def ask_load(i):
        u = flip(v, i, var)
        return pltpu.make_async_copy(ask.at[u], ask_s.at[u], ask_l.at[i])

    def z_copy(i, k):
        u = flip(v, i, var)
        return remote(far.at[u, k], farz.at[v, k], z_s.at[i, k], z_r.at[i, k], var=u)

    def cc_copy(b, k):
        return remote(cc_out.at[b, k], cc_in.at[b, s], cc_s.at[b, k], cc_r.at[b, s], samp=k)

    def oo_copy(b, k):
        return remote(oo_out.at[b, k], oo_in.at[b, s], oo_s.at[b, k], oo_r.at[b, s], samp=k)

    def cc_arrival(b, k):
        return remote(cc_out.at[b, k], cc_in.at[b, k], cc_s.at[b, k], cc_r.at[b, k], samp=k)

    def oo_arrival(b, k):
        return remote(oo_out.at[b, k], oo_in.at[b, k], oo_s.at[b, k], oo_r.at[b, k], samp=k)

    def out_copy(d, b):
        return remote(fin_ref.at[s, b], fin_ref.at[s, b], out_s.at[d, b], out_r.at[d, b],
                      samp=flip(s, d, samp))

    def near_panel(u, k):
        return x[lax.shift_right_logical(tab[u, 0, k], bits) & (cols - 1)]

    def gram(left, right):
        return lax.dot_general(left, right, over_first, preferred_element_type=jnp.float32)

    row_at = lax.broadcasted_iota(jnp.int32, (width, width), 0)
    col_at = lax.broadcasted_iota(jnp.int32, (width, width), 1)
    eye = row_at == col_at
    fold_row = lax.broadcasted_iota(jnp.int32, (fold_rows, width), 0)
    fold_col = lax.broadcasted_iota(jnp.int32, (fold_rows, width), 1)
    from_top = fold_col >= fold_row + fold_rows
    own_top = (fold_col < fold_rows) & (fold_col >= fold_row)
    note_row = lax.broadcasted_iota(jnp.int32, (16, width), 0)

    def folded(part):
        return jnp.where(from_top, pltpu.roll(part[:fold_rows], fold_rows, 1), part[fold_rows:])

    def unfolded(half_block, diag):
        turned = pltpu.roll(half_block, fold_rows, 1)
        mirror = jnp.concatenate([half_block, turned], axis=0).T
        top = jnp.where(own_top, turned, mirror[fold_rows:])
        bottom = jnp.where(from_top, mirror[:fold_rows], half_block)
        return jnp.where(eye, diag, jnp.concatenate([top, bottom], axis=0))

    def diagonal_of(part):
        return jnp.sum(jnp.where(eye, part, 0.0), axis=0, keepdims=True)

    def note_of(diag):
        high = diag.astype(jnp.bfloat16).astype(jnp.float32)
        return jnp.where(note_row == 0, high, jnp.where(note_row == 1, diag - high, 0.0))

    def start_cc(b):
        for k in range(samp):
            u = flip(v, partner(v, b, k, var), var)
            c = near_panel(u, k)
            part = gram(c, c)
            short, diag = folded(part), diagonal_of(part)
            cc_out[b, k, :fold_rows] = short.astype(jnp.bfloat16)
            cc_out[b, k, fold_rows:] = note_of(diag).astype(jnp.bfloat16)

            @pl.when(s == k)
            def _():
                cc_own[b] = short
                cc_diag[b] = diag

            @pl.when(s != k)
            def _():
                cc_copy(b, k).start()

    def start_oo(b, ranks, far_panel):
        for k in ranks:
            u = flip(v, partner(v, b, k, var), var)
            o = far_panel(u, k)
            part = gram(o, jnp.concatenate([near_panel(u, k), o], axis=1))
            cross, own = part[:, :width], part[:, width:]
            short, diag = folded(own), diagonal_of(own)
            oo_out[b, k, :width] = cross.astype(jnp.bfloat16)
            oo_out[b, k, width:width + fold_rows] = short.astype(jnp.bfloat16)
            oo_out[b, k, width + fold_rows:] = note_of(diag).astype(jnp.bfloat16)

            @pl.when(s == k)
            def _():
                oc_own[b] = cross
                oo_own[b] = short
                oo_diag[b] = diag

            @pl.when(s != k)
            def _():
                oo_copy(b, k).start()

    def arrived(b, ranks):
        for k in ranks:
            z_copy(partner(v, b, k, var), k).wait_recv()

    def note_sum(note):
        note = note.astype(jnp.float32)
        return note[0:1] + note[1:2]

    def column(b):
        for d in range(1, samp):
            cc_arrival(b, flip(s, d, samp)).wait_recv()
            oo_arrival(b, flip(s, d, samp)).wait_recv()
        cc, oc, oo = cc_own[b], oc_own[b], oo_own[b]
        cc_d, oo_d = cc_diag[b], oo_diag[b]
        for d in range(1, samp):
            p = flip(s, d, samp)
            cc = cc + cc_in[b, p, :fold_rows].astype(jnp.float32)
            cc_d = cc_d + note_sum(cc_in[b, p, fold_rows:])
            oc = oc + oo_in[b, p, :width].astype(jnp.float32)
            oo = oo + oo_in[b, p, width:width + fold_rows].astype(jnp.float32)
            oo_d = oo_d + note_sum(oo_in[b, p, width + fold_rows:])
        cc, oo = unfolded(cc, cc_d), unfolded(oo, oo_d)
        both = jnp.concatenate(
            [jnp.concatenate([cc, oc.T], axis=1), jnp.concatenate([oc, oo], axis=1)], axis=0)
        high = both.astype(jnp.bfloat16)
        low = (both - high.astype(jnp.float32)).astype(jnp.bfloat16)
        gram_parts = jnp.concatenate([high, low], axis=1)
        u = flip(v, partner(v, b, s, var), var)
        value = tab[u, 0, s]
        col = lax.shift_right_logical(value, bits) & (cols - 1)
        slot = lax.shift_right_logical(value, 2 * bits) & 1
        wd = jnp.where(eye, 0.0, blk[col, slot])
        wo = blk[col, 1 - slot]
        dv = dia_ref[col]
        for step in range(STEPS):
            rounded = jnp.concatenate(
                [jnp.where(eye, dv, wd).astype(jnp.bfloat16), wo.astype(jnp.bfloat16)], axis=0)
            grad = jnp.dot(gram_parts, jnp.concatenate([rounded, rounded], axis=0),
                           preferred_element_type=jnp.float32)
            squares = jnp.sum(grad * rounded.astype(jnp.float32), axis=0, keepdims=True)
            terms = (squares / (2.0 * total_rows) - jnp.log(dv)
                     + penalty * jnp.sum(jnp.abs(wd) + jnp.abs(wo), axis=0, keepdims=True))
            acc[step:step + 1, :] += terms
            grad = grad / total_rows
            gd, go = grad[:width], grad[width:]
            wo = shrink(wo - step_length * go, step_length * penalty)
            wd = jnp.where(eye, 0.0, shrink(wd - step_length * gd, step_length * penalty))
            along = jnp.sum(jnp.where(eye, gd, 0.0), axis=0, keepdims=True)
            moved = dv - step_length * along
            dv = 0.5 * (moved + jnp.sqrt(moved * moved + 4.0 * step_length))
        fin_ref[s, b, 0] = wd.astype(jnp.bfloat16)
        fin_ref[s, b, 1] = wo.astype(jnp.bfloat16)
        tails_ref[s, pl.ds(b, 1), :] = dv

    def send_out(b, direct):
        for d in range(1, samp if direct else samp - 1):
            out_copy(d, b).start()

    def relay_copy(part, b):
        near, to = flip(s, 1 + part, samp), flip(s, 2 - part, samp)
        return remote(fin_ref.at[near, b, part], fin_ref.at[near, b, part],
                      rel_s.at[part, b], rel_r.at[part, b], samp=to)

    def relay(b):
        for part in range(2):
            out_copy(1 + part, b).wait_recv()
            relay_copy(part, b).start()

    close = half + 2 * inner
    distant = 2 * half + 2 - close
    asks = [2, 3, close, close + 1, 1, distant, distant + 1]
    for i in asks:
        ask_copy(i).start()
    acc[...] = jnp.zeros_like(acc)
    for x_load in x_loads:
        x_load.wait()
    blk_load.start()
    dia_load.start()
    tab_load.wait()
    start_cc(0)

    def learn(offsets):
        for i in offsets:
            ask_copy(i).wait_recv()
            ask_load(i).start()
        for i in offsets:
            ask_load(i).wait()

    def send_panel(i, k):
        u = flip(v, i, var)
        far[u, k] = x[ask_s[u, 0, k] & (cols - 1)]
        z_copy(i, k).start()

    def send_across():
        for n in range(samp):
            for i in (close, distant, close + 1, distant + 1):
                send_panel(i, send_rank(i, n, samp, half))

    learn([2, 3, close, close + 1])

    @pl.when(inner == 1)
    def _():
        for i in (close, close + 1):
            send_panel(i, send_rank(i, 0, samp, half))

    for n in range(samp):
        for i in (2, 3):
            send_panel(i, send_rank(i, n, samp, half))
    learn([1, distant, distant + 1])

    @pl.when(inner == 1)
    def _():
        for i in (distant, distant + 1):
            send_panel(i, send_rank(i, 0, samp, half))
        for n in range(1, samp):
            for i in (close, distant, close + 1, distant + 1):
                send_panel(i, send_rank(i, n, samp, half))

    for k in range(samp):
        send_panel(1, k)

    every = range(samp)
    start_oo(0, every, lambda u, k: x[tab[u, 0, k] & (cols - 1)])
    start_cc(1)

    def from_var(u, k):
        return farz[u, k]

    def take(b, ranks=every):
        arrived(b, ranks)
        start_oo(b, ranks, from_var)

    def settle(b, direct=False):
        column(b)
        send_out(b, direct)

    last = var - 1
    take(1)
    for b in range(2, var):
        start_cc(b)
    blk_load.wait()
    dia_load.wait()
    settle(0)
    take(2)
    settle(1)
    arrived(3, every)

    @pl.when(inner == 0)
    def _():
        send_across()

    start_oo(3, every, from_var)
    settle(2)
    relay(0)
    relay(1)
    take(4)
    settle(3)
    relay(2)
    take(5)
    settle(4)
    relay(3)
    settle(5)
    relay(4)
    take(6)
    relay(5)
    settle(6, True)
    take(last, range(samp // 2))
    take(last, range(samp // 2, samp))
    column(last)

    tails_ref[s, var:, :] = acc[...]

    def tail_copy(d):
        return remote(tails_ref.at[s], tails_ref.at[s], tail_s.at[d], tail_r.at[d],
                      samp=flip(s, d, samp))

    def oz_copy(i):
        return remote(oz.at[v], oz.at[v], oz_s.at[i], oz_r.at[i], var=flip(v, i, var))

    for d in range(1, samp):
        tail_copy(d).start()
    send_out(last, True)
    for d in range(1, samp):
        tail_copy(d).wait_recv()
    group = tails_ref[0, var:, :]
    for k in range(1, samp):
        group = group + tails_ref[k, var:, :]
    oz[v] = group
    for i in range(1, var):
        oz_copy(i).start()

    def finish(b, carry):
        for d in range(1, samp - 1):
            out_copy(d, b).wait_send()
        return carry

    def finish_relay(b, carry):
        for part in range(2):
            relay_copy(part, b).wait()
        return carry

    lax.fori_loop(0, var, finish, 0)
    for k in range(samp):
        @pl.when(s != k)
        def _():
            def sent(b, carry):
                cc_copy(b, k).wait_send()
                oo_copy(b, k).wait_send()
                return carry

            lax.fori_loop(0, var, sent, 0)
    lax.fori_loop(0, var - 2, finish_relay, 0)
    for b in range(var - 2, var):
        for d in range(1, samp - 1):
            out_copy(d, b).wait_recv()
        out_copy(samp - 1, b).wait()
    for d in range(1, samp):
        tail_copy(d).wait_send()
    for i in range(1, var):
        ask_copy(i).wait_send()
        for k in range(samp):
            z_copy(i, k).wait_send()
    for i in range(1, var):
        oz_copy(i).wait()
    whole = oz[0]
    for u in range(1, var):
        whole = whole + oz[u]
    obj_ref[...] = whole


def unpack_kernel(samp, var, order, bits, table, fin_ref, tails_ref, whole_ref,
                  out_hbm, dia_ref, obj_ref, stage, sem):
    v = lax.axis_index("var")
    last = (1 << bits) - 1
    copies = []
    for b in range(var):
        for k in range(samp):
            value = table[flip(v, partner(v, b, k, var), var), 0, k]
            col = lax.shift_right_logical(value, bits) & last
            slot = lax.shift_right_logical(value, 2 * bits) & 1
            stage[b, k, slot] = fin_ref[k, b, 0].astype(jnp.float32)
            stage[b, k, 1 - slot] = fin_ref[k, b, 1].astype(jnp.float32)
            copy = pltpu.make_async_copy(stage.at[b, k], out_hbm.at[col], sem.at[b, k])
            copy.start()
            copies.append(copy)
            dia_ref[pl.ds(col, 1), :] = tails_ref[k, b:b + 1, :]
    for step in range(STEPS):
        obj_ref[step] = jnp.sum(whole_ref[step:step + 1, :]) / order
    for copy in copies:
        copy.wait()


def column_body(observed, blocks, diagonal, pattern):
    cols, width = blocks.shape[0], blocks.shape[2]
    rows = observed.shape[0]
    var, samp = lax.axis_size("var"), lax.axis_size("samp")
    bits = cols.bit_length() - 1

    vmem = pl.BlockSpec(memory_space=pltpu.VMEM)
    smem = pl.BlockSpec(memory_space=pltpu.SMEM)
    hbm = pl.BlockSpec(memory_space=pltpu.HBM)
    dma = pltpu.SemaphoreType.DMA
    bf16, f32 = jnp.bfloat16, jnp.float32
    fold, late_rows = width // 2 + 16, width + width // 2 + 16
    fin, tails, whole, table = pl.pallas_call(
        functools.partial(main_kernel, samp, var),
        out_shape=(
            jax.ShapeDtypeStruct((samp, var, 2, width, width), bf16),
            jax.ShapeDtypeStruct((samp, var + 8, width), f32),
            jax.ShapeDtypeStruct((8, width), f32),
            jax.ShapeDtypeStruct((var, 1, width), jnp.int32),
        ),
        in_specs=[hbm] * 4,
        out_specs=(vmem,) * 4,
        scratch_shapes=[
            pltpu.VMEM((2, cols), jnp.int32),
            pltpu.VMEM((cols, rows, width), observed.dtype),
            pltpu.VMEM(blocks.shape, f32),
            pltpu.VMEM((cols, 1, width), f32),
            pltpu.SMEM((var, 1, width), jnp.int32),
            pltpu.VMEM((var, 1, width), jnp.int32),
            pltpu.SMEM((var, 1, width), jnp.int32),
            pltpu.VMEM((var, samp, rows, width), observed.dtype),
            pltpu.VMEM((var, samp, rows, width), observed.dtype),
            pltpu.VMEM((var, samp, fold, width), bf16),
            pltpu.VMEM((var, samp, fold, width), bf16),
            pltpu.VMEM((var, width // 2, width), f32),
            pltpu.VMEM((var, 1, width), f32),
            pltpu.VMEM((var, samp, late_rows, width), bf16),
            pltpu.VMEM((var, samp, late_rows, width), bf16),
            pltpu.VMEM((var, width, width), f32),
            pltpu.VMEM((var, width // 2, width), f32),
            pltpu.VMEM((var, 1, width), f32),
            pltpu.VMEM((var, 8, width), f32),
            pltpu.VMEM((8, width), f32),
            dma((cols + 3,)), dma, dma((var,)), dma((var,)), dma((var,)),
            dma((var, samp)), dma((var, samp)), dma((var, samp)), dma((var, samp)),
            dma((var, samp)), dma((var, samp)), dma((samp, var)), dma((samp, var)),
            dma((2, var)), dma((2, var)), dma((samp,)), dma((samp,)), dma((var,)), dma((var,)),
        ],
        compiler_params=pltpu.CompilerParams(
            collective_id=0, has_side_effects=True, vmem_limit_bytes=40 * 2 ** 20),
        name="columns",
    )(*(pltpu.with_memory_space_constraint(array, pltpu.HBM)
        for array in (pattern.T, observed, blocks, diagonal.reshape(cols, 1, width))))

    new_blocks, new_diagonal, objective = pl.pallas_call(
        functools.partial(unpack_kernel, samp, var, float(cols * width * var), bits),
        out_shape=(
            jax.ShapeDtypeStruct(blocks.shape, f32),
            jax.ShapeDtypeStruct((cols, width), f32),
            jax.ShapeDtypeStruct((STEPS,), f32),
        ),
        in_specs=[smem, vmem, vmem, vmem],
        out_specs=(hbm, vmem, smem),
        scratch_shapes=[
            pltpu.VMEM((var, samp, 2, width, width), f32),
            dma((var, samp)),
        ],
        compiler_params=pltpu.CompilerParams(vmem_limit_bytes=16 * 2 ** 20),
        name="unpack",
    )(table, fin, tails, whole)
    return new_blocks, new_diagonal.reshape(-1), objective


def advance(diag_block, off_block, diag_values, grad_diag, grad_off, diag_mask, total_rows):
    grad_diag = grad_diag / total_rows
    grad_off = grad_off / total_rows
    new_off = shrink(off_block - step_length * grad_off, step_length * penalty)
    new_diag_block = jnp.where(
        diag_mask, 0.0, shrink(diag_block - step_length * grad_diag, step_length * penalty)
    )
    along = jnp.sum(jnp.where(diag_mask, grad_diag, 0.0), axis=1)
    moved = diag_values - step_length * along
    new_values = 0.5 * (moved + jnp.sqrt(moved * moved + 4.0 * step_length))
    return (new_diag_block, new_off, new_values)


def body(observed, blocks, diagonal, pattern):
    col_count = blocks.shape[0]
    block_width = blocks.shape[2]
    sample_rows = observed.shape[0]
    var_count = lax.axis_size("var")
    samp_count = lax.axis_size("samp")
    capacity = max(2, -(-col_count // var_count))
    total_rows = sample_rows * samp_count
    matrix_order = col_count * block_width * var_count
    var_index = lax.axis_index("var")
    column_ids = jnp.arange(col_count, dtype=jnp.int32)
    columns = var_index * col_count + column_ids
    on_diag = pattern == columns[:, None]
    off_row = jnp.sum(jnp.where(on_diag, 0, pattern), axis=1)
    owner_index = off_row // col_count
    resident_block = off_row % col_count
    earlier = (owner_index[None, :] == owner_index[:, None]) & (
        column_ids[None, :] < column_ids[:, None]
    )
    position_rank = jnp.sum(earlier, axis=1)
    slot_index = owner_index * capacity + position_rank
    all_slots = jnp.arange(var_count * capacity, dtype=jnp.int32)
    slot_match = slot_index[:, None] == all_slots[None, :]
    wanted = jnp.sum(jnp.where(slot_match, resident_block[:, None], 0), axis=0)
    asked_blocks = lax.all_to_all(wanted, "var", split_axis=0, concat_axis=0, tiled=True)
    nearby_panels = observed.reshape(sample_rows, col_count, block_width)
    outgoing = jnp.take(nearby_panels, asked_blocks, axis=1)
    arrived = lax.all_to_all(outgoing, "var", split_axis=1, concat_axis=1, tiled=True)
    distant_panels = jnp.take(arrived, slot_index, axis=1)
    diag_mask = jnp.eye(block_width, dtype=bool)
    flags = on_diag[:, :, None, None]
    diag_block = jnp.sum(jnp.where(flags, blocks, 0.0), axis=1)
    diag_block = jnp.where(diag_mask, 0.0, diag_block)
    off_block = jnp.sum(jnp.where(flags, 0.0, blocks), axis=1)
    diag_values = diagonal.reshape(col_count, block_width)
    samp_first = (lax.axis_index("samp") == 0).astype(jnp.float32)
    objective_parts = []
    for iteration in range(STEPS):
        full_diag = jnp.where(diag_mask, diag_values[:, None, :], diag_block)
        product = jnp.einsum(
            "qlh,lhy->qly",
            nearby_panels,
            full_diag.astype(jnp.bfloat16),
            preferred_element_type=jnp.float32,
        )
        product = product + jnp.einsum(
            "qlh,lhy->qly",
            distant_panels,
            off_block.astype(jnp.bfloat16),
            preferred_element_type=jnp.float32,
        )
        squares = jnp.sum(product * product)
        local_terms = -jnp.sum(jnp.log(diag_values)) + penalty * (
            jnp.sum(jnp.abs(diag_block)) + jnp.sum(jnp.abs(off_block))
        )
        part_value = (squares / (2.0 * total_rows) + samp_first * local_terms) / matrix_order
        objective_parts.append(part_value)
        lower_precision_product = product.astype(jnp.bfloat16)
        grad_diag = jnp.einsum(
            "rei,reo->eio",
            nearby_panels,
            lower_precision_product,
            preferred_element_type=jnp.float32,
        )
        grad_off = jnp.einsum(
            "rei,reo->eio",
            distant_panels,
            lower_precision_product,
            preferred_element_type=jnp.float32,
        )
        grad_diag, grad_off = lax.psum((grad_diag, grad_off), "samp")
        diag_block, off_block, diag_values = advance(
            diag_block, off_block, diag_values, grad_diag, grad_off, diag_mask, total_rows
        )
    objective = lax.psum(jnp.stack(objective_parts), ("samp", "var"))
    new_blocks = jnp.where(flags, diag_block[:, None], off_block[:, None])
    return (new_blocks, diag_values.reshape(-1), objective)


def power_of_two(count):
    return count & (count - 1) == 0


def whole_body(observed, blocks, diagonal, pattern):
    cols = blocks.shape[0]
    var, samp = lax.axis_size("var"), lax.axis_size("samp")
    exact = samp == 4 and samp * var == cols and var == 2 * samp and blocks.shape[2] == 128
    if exact and power_of_two(samp) and power_of_two(var):
        return column_body(observed, blocks, diagonal, pattern)
    return body(observed, blocks, diagonal, pattern)


def solution(mesh):
    placed = (P("samp", "var"), P("var", None, None, None), P("var"), P("var", None))
    return jax.shard_map(
        whole_body,
        mesh=mesh,
        in_specs=placed,
        out_specs=(P("var", None, None, None), P("var"), P()),
        check_vma=False,
    )
```

```python
import functools

import jax
import jax.numpy as jnp
from jax import lax
from jax.experimental import pallas as pl
from jax.experimental.pallas import tpu as pltpu
from jax.sharding import PartitionSpec as P

STEPS = 2


step_length = 0.5
penalty = 0.5
MESH = pl.DeviceIdType.MESH


def shrink(moved, level):
    return moved - jnp.clip(moved, -level, level)


def mates(s):
    return s, s + 1 - 2 * (s % 2), s + 2 - 4 * (s // 2), 3 - s


def places(v):
    far_half = 1 - v // 4
    own = v // 2
    return 2 * own, 2 * (own + 1 - 2 * (own % 2)), 2 + 2 * far_half, 6 * far_half


OWN, NEXT, CLOSE, DISTANT = range(4)


def batch_place(b, high, low):
    return ((OWN, 0), (OWN, 1), (NEXT, high), (CLOSE, low), (NEXT, 1 - high),
            (DISTANT, low), (DISTANT, 1 - low), (CLOSE, 1 - low))[b]


def batch_owner(v, bases, b, k):
    chip, other = batch_place(b, k // 2, k % 2)
    return bases[chip] + (v % 2 + other) % 2


def send_rank(chip, other, n):
    if chip == NEXT:
        return (n + 2 * other) % 4
    return 2 * n + other if n < 2 else 2 * (n - 2) + 1 - other


def main_kernel(samp, var, pat_hbm, x_hbm, blk_hbm, dia_hbm,
                fin_ref, tails_ref, obj_ref, tab_ref,
                pat_ref, x, blk, dia_ref, tab, ask_s, far, farz, cc_out, cc_in, cc_own, cc_diag,
                oo_out, oo_in, oc_own, oo_own, oo_diag, oz, acc,
                load, tab_l, ask_ss, ask_rs, cc_s, cc_r, z_s, z_r, oo_s, oo_r, out_s, out_r,
                rel_s, rel_r, tail_s, tail_r, oz_s, oz_r):
    s = lax.axis_index("samp")
    v = lax.axis_index("var")
    inner = (v // 2 + v // 4) % 2
    core = v % 2
    bases = places(v)
    cores = (core, 1 - core)
    mate = mates(s)
    spots = [(chip, other) for chip in range(4) for other in range(2)][1:]
    rows, width = x.shape[1], x.shape[2]
    fold_rows = width // 2
    total_rows = rows * samp
    over_first = (((0,), (0,)), ((), ()))

    cols = x.shape[0]
    bits = cols.bit_length() - 1
    barrier = pltpu.get_barrier_semaphore()
    for chip, other in spots:
        pl.semaphore_signal(barrier, inc=1, device_id={"var": bases[chip] + cores[other]}, device_id_type=MESH)
    for d in range(1, samp):
        pl.semaphore_signal(barrier, inc=1, device_id={"samp": mate[d]}, device_id_type=MESH)

    pat_load = pltpu.make_async_copy(pat_hbm, pat_ref, load.at[cols + 1])
    pat_load.start()
    x_loads = [
        pltpu.make_async_copy(x_hbm.at[:, l * width:(l + 1) * width], x.at[l], load.at[l])
        for l in range(cols)
    ]
    for x_load in x_loads:
        x_load.start()
    blk_load = pltpu.make_async_copy(blk_hbm, blk, load.at[cols])
    dia_load = pltpu.make_async_copy(dia_hbm, dia_ref, load.at[cols + 2])

    pat_load.wait()
    first, second = pat_ref[0:1, :], pat_ref[1:2, :]
    ids = lax.broadcasted_iota(jnp.int32, (1, cols), 1)
    lead = first == v * cols + ids
    off_row = jnp.where(lead, second, first)
    owner = lax.shift_right_logical(off_row, bits)
    entry = (off_row & (cols - 1)) + ids * cols + jnp.where(lead, 0, cols * cols)
    below = lax.broadcasted_iota(jnp.int32, (cols, cols), 0)
    across = lax.broadcasted_iota(jnp.int32, (cols, cols), 1)
    wide = jnp.broadcast_to(owner, (cols, cols))
    down = jnp.sum(jnp.where(below == across, wide, 0), axis=1, keepdims=True)
    rank = jnp.sum(jnp.where((down == wide) & (below < across), 1, 0), axis=0, keepdims=True)
    mine = lax.broadcasted_iota(jnp.int32, (var, cols), 0) == owner
    lanes = lax.broadcasted_iota(jnp.int32, (var, width), 1)
    table = jnp.zeros((var, width), jnp.int32)
    for k in range(samp):
        picked = jnp.sum(jnp.where(mine & (rank == k), entry, 0), axis=1, keepdims=True)
        table = jnp.where(lanes == k, picked, table)
    for u in range(var):
        tab_ref[u] = table[u:u + 1, :]
    tab_load = pltpu.make_async_copy(tab_ref, tab, tab_l)
    tab_load.start()

    pl.semaphore_wait(barrier, samp + var - 2)

    def remote(src, dst, send, recv, **where):
        return pltpu.make_async_remote_copy(
            src_ref=src, dst_ref=dst, send_sem=send, recv_sem=recv,
            device_id=where, device_id_type=MESH)

    def place(spot):
        return bases[spot[0]] + cores[spot[1]]

    def ask_copy(u):
        return remote(tab_ref.at[u], ask_s.at[v], ask_ss.at[u], ask_rs.at[v], var=u)

    def ask_arrival(u):
        return remote(tab_ref.at[u], ask_s.at[u], ask_ss.at[u], ask_rs.at[u], var=u)

    def z_copy(u, k):
        return remote(far.at[u, k], farz.at[v, k], z_s.at[u, k], z_r.at[v, k], var=u)

    def z_arrival(u, k):
        return remote(far.at[u, k], farz.at[u, k], z_s.at[u, k], z_r.at[u, k], var=u)

    def cc_copy(b, k):
        return remote(cc_out.at[b, k], cc_in.at[b, s], cc_s.at[b, k], cc_r.at[b, s], samp=k)

    def oo_copy(b, k):
        return remote(oo_out.at[b, k], oo_in.at[b, s], oo_s.at[b, k], oo_r.at[b, s], samp=k)

    def cc_arrival(b, k):
        return remote(cc_out.at[b, k], cc_in.at[b, k], cc_s.at[b, k], cc_r.at[b, k], samp=k)

    def oo_arrival(b, k):
        return remote(oo_out.at[b, k], oo_in.at[b, k], oo_s.at[b, k], oo_r.at[b, k], samp=k)

    def out_copy(d, b):
        return remote(fin_ref.at[s, b], fin_ref.at[s, b], out_s.at[d, b], out_r.at[d, b],
                      samp=mate[d])

    def near_panel(u, k):
        return x[lax.shift_right_logical(tab[u, 0, k], bits) & (cols - 1)]

    def gram(left, right):
        return lax.dot_general(left, right, over_first, preferred_element_type=jnp.float32)

    row_at = lax.broadcasted_iota(jnp.int32, (width, width), 0)
    col_at = lax.broadcasted_iota(jnp.int32, (width, width), 1)
    eye = row_at == col_at
    fold_row = lax.broadcasted_iota(jnp.int32, (fold_rows, width), 0)
    fold_col = lax.broadcasted_iota(jnp.int32, (fold_rows, width), 1)
    from_top = fold_col >= fold_row + fold_rows
    own_top = (fold_col < fold_rows) & (fold_col >= fold_row)
    note_row = lax.broadcasted_iota(jnp.int32, (16, width), 0)

    def folded(part):
        return jnp.where(from_top, pltpu.roll(part[:fold_rows], fold_rows, 1), part[fold_rows:])

    def unfolded(half_block, diag):
        turned = pltpu.roll(half_block, fold_rows, 1)
        mirror = jnp.concatenate([half_block, turned], axis=0).T
        top = jnp.where(own_top, turned, mirror[fold_rows:])
        bottom = jnp.where(from_top, mirror[:fold_rows], half_block)
        return jnp.where(eye, diag, jnp.concatenate([top, bottom], axis=0))

    def diagonal_of(part):
        return jnp.sum(jnp.where(eye, part, 0.0), axis=0, keepdims=True)

    def note_of(diag):
        high = diag.astype(jnp.bfloat16).astype(jnp.float32)
        return jnp.where(note_row == 0, high, jnp.where(note_row == 1, diag - high, 0.0))

    def start_cc(b):
        for k in range(samp):
            u = batch_owner(v, bases, b, k)
            c = near_panel(u, k)
            part = gram(c, c)
            short, diag = folded(part), diagonal_of(part)
            cc_out[b, k, :fold_rows] = short.astype(jnp.bfloat16)
            cc_out[b, k, fold_rows:] = note_of(diag).astype(jnp.bfloat16)

            @pl.when(s == k)
            def _():
                cc_own[b] = short
                cc_diag[b] = diag

            @pl.when(s != k)
            def _():
                cc_copy(b, k).start()

    def start_oo(b, ranks, far_panel):
        for k in ranks:
            u = batch_owner(v, bases, b, k)
            o = far_panel(u, k)
            part = gram(o, jnp.concatenate([near_panel(u, k), o], axis=1))
            cross, own = part[:, :width], part[:, width:]
            short, diag = folded(own), diagonal_of(own)
            oo_out[b, k, :width] = cross.astype(jnp.bfloat16)
            oo_out[b, k, width:width + fold_rows] = short.astype(jnp.bfloat16)
            oo_out[b, k, width + fold_rows:] = note_of(diag).astype(jnp.bfloat16)

            @pl.when(s == k)
            def _():
                oc_own[b] = cross
                oo_own[b] = short
                oo_diag[b] = diag

            @pl.when(s != k)
            def _():
                oo_copy(b, k).start()

    def arrived(b, ranks):
        for k in ranks:
            z_arrival(batch_owner(v, bases, b, k), k).wait_recv()

    def note_sum(note):
        note = note.astype(jnp.float32)
        return note[0:1] + note[1:2]

    def column(b):
        for d in range(1, samp):
            cc_arrival(b, mate[d]).wait_recv()
            oo_arrival(b, mate[d]).wait_recv()
        cc, oc, oo = cc_own[b], oc_own[b], oo_own[b]
        cc_d, oo_d = cc_diag[b], oo_diag[b]
        for d in range(1, samp):
            p = mate[d]
            cc = cc + cc_in[b, p, :fold_rows].astype(jnp.float32)
            cc_d = cc_d + note_sum(cc_in[b, p, fold_rows:])
            oc = oc + oo_in[b, p, :width].astype(jnp.float32)
            oo = oo + oo_in[b, p, width:width + fold_rows].astype(jnp.float32)
            oo_d = oo_d + note_sum(oo_in[b, p, width + fold_rows:])
        cc, oo = unfolded(cc, cc_d), unfolded(oo, oo_d)
        both = jnp.concatenate(
            [jnp.concatenate([cc, oc.T], axis=1), jnp.concatenate([oc, oo], axis=1)], axis=0)
        high = both.astype(jnp.bfloat16)
        low = (both - high.astype(jnp.float32)).astype(jnp.bfloat16)
        gram_parts = jnp.concatenate([high, low], axis=1)
        u = batch_owner(v, bases, b, s)
        value = tab[u, 0, s]
        col = lax.shift_right_logical(value, bits) & (cols - 1)
        slot = lax.shift_right_logical(value, 2 * bits) & 1
        wd = jnp.where(eye, 0.0, blk[col, slot])
        wo = blk[col, 1 - slot]
        dv = dia_ref[col]
        for step in range(STEPS):
            rounded = jnp.concatenate(
                [jnp.where(eye, dv, wd).astype(jnp.bfloat16), wo.astype(jnp.bfloat16)], axis=0)
            grad = jnp.dot(gram_parts, jnp.concatenate([rounded, rounded], axis=0),
                           preferred_element_type=jnp.float32)
            squares = jnp.sum(grad * rounded.astype(jnp.float32), axis=0, keepdims=True)
            terms = (squares / (2.0 * total_rows) - jnp.log(dv)
                     + penalty * jnp.sum(jnp.abs(wd) + jnp.abs(wo), axis=0, keepdims=True))
            acc[step:step + 1, :] += terms
            grad = grad / total_rows
            gd, go = grad[:width], grad[width:]
            wo = shrink(wo - step_length * go, step_length * penalty)
            wd = jnp.where(eye, 0.0, shrink(wd - step_length * gd, step_length * penalty))
            along = jnp.sum(jnp.where(eye, gd, 0.0), axis=0, keepdims=True)
            moved = dv - step_length * along
            dv = 0.5 * (moved + jnp.sqrt(moved * moved + 4.0 * step_length))
        lead = slot == 0
        fin_ref[s, b, 0] = jnp.where(lead, wd, wo).astype(jnp.bfloat16)
        fin_ref[s, b, 1] = jnp.where(lead, wo, wd).astype(jnp.bfloat16)
        tails_ref[s, pl.ds(b, 1), :] = dv

    def relay_copy(part, b):
        near, to = mate[1 + part], mate[2 - part]
        return remote(fin_ref.at[near, b, part], fin_ref.at[near, b, part],
                      rel_s.at[part, b], rel_r.at[part, b], samp=to)

    def relay(b):
        for part in range(2):
            out_copy(1 + part, b).wait_recv()
            relay_copy(part, b).start()

    close = [(CLOSE, 0), (CLOSE, 1)]
    beside = [(NEXT, 0), (NEXT, 1)]
    distant = [(DISTANT, 0), (DISTANT, 1)]
    for spot in close + beside + distant + [(OWN, 1)]:
        ask_copy(place(spot)).start()
    acc[...] = jnp.zeros_like(acc)
    for x_load in x_loads:
        x_load.wait()
    blk_load.start()
    dia_load.start()
    tab_load.wait()
    start_cc(0)

    def learn(wanted):
        for spot in wanted:
            ask_arrival(place(spot)).wait_recv()

    def send_panel(spot, k):
        u = place(spot)
        far[u, k] = x[ask_s[u, 0, k] & (cols - 1)]
        z_copy(u, k).start()

    def send(wanted, turns):
        for n in turns:
            for spot in wanted:
                send_panel(spot, send_rank(*spot, n))

    across = [close[0], distant[0], close[1], distant[1]]

    @pl.when(inner == 1)
    def _():
        learn(close)
        send(close, [0])
        learn(distant + beside)
        send(distant, [0])
        send(beside, range(samp))
        send(across, range(1, samp))

    @pl.when(inner == 0)
    def _():
        learn(beside)
        send(beside, range(samp))
        learn(close + distant)

    learn([(OWN, 1)])
    for k in range(samp):
        send_panel((OWN, 1), k)

    every = range(samp)
    start_oo(0, every, lambda u, k: x[tab[u, 0, k] & (cols - 1)])
    start_cc(1)

    def from_var(u, k):
        return farz[u, k]

    def take(b, ranks=every):
        arrived(b, ranks)
        start_oo(b, ranks, from_var)

    def settle(b):
        column(b)
        for d in range(1, samp - 1):
            out_copy(d, b).start()

    last = var - 1
    take(1)
    for b in range(2, var):
        start_cc(b)
    blk_load.wait()
    dia_load.wait()
    settle(0)
    take(2)
    arrived(3, every)

    @pl.when(inner == 0)
    def _():
        send(across, range(samp))

    settle(1)
    start_oo(3, every, from_var)
    settle(2)
    relay(0)
    relay(1)
    take(4)
    settle(3)
    relay(2)
    take(5)
    settle(4)
    relay(3)
    settle(5)
    relay(4)
    take(6)
    relay(5)
    take(last, range(samp // 2))
    settle(6)
    take(last, range(samp // 2, samp))
    relay(last - 1)
    column(last)

    def tail_copy(d):
        return remote(tails_ref.at[s], tails_ref.at[s], tail_s.at[d], tail_r.at[d],
                      samp=mate[d])

    def oz_copy(d, u):
        return remote(oz.at[s * var + v], oz.at[s * var + v], oz_s.at[mate[d] * var + u], oz_r.at[s * var + v],
                      samp=mate[d], var=u)

    def oz_arrival(d, u):
        at = mate[d] * var + u
        return remote(oz.at[at], oz.at[at], oz_s.at[at], oz_r.at[at], samp=mate[d], var=u)

    halves = [acc[step:step + 1, :] + pltpu.roll(acc[step:step + 1, :], fold_rows, 1) for step in range(STEPS)]
    oz[s * var + v] = jnp.where(fold_col[:1] < fold_rows, halves[0], halves[1])
    peers = [(d, place(spot)) for d in range(samp - 1, -1, -1) for spot in spots[::-1] + [(OWN, 0)]][:-1]
    for peer in peers:
        oz_copy(*peer).start()
    for d in range(1, samp - 1):
        out_copy(d, last).start()

    early_owner = s < samp // 2
    late_owner = s >= samp // 2

    @pl.when(late_owner)
    def _():
        out_copy(samp - 1, last).start()

    for d in range(1, samp):
        tail_copy(d).start()

    @pl.when(early_owner)
    def _():
        out_copy(1, last).wait_recv()
        relay_copy(0, last).start()
        out_copy(2, last).wait_recv()

    @pl.when(late_owner)
    def _():
        out_copy(2, last).wait_recv()
        relay_copy(1, last).start()
        out_copy(1, last).wait_recv()

    def finish(b, carry):
        for d in range(1, samp - 1):
            out_copy(d, b).wait_send()
        return carry

    def finish_relay(b, carry):
        for part in range(2):
            relay_copy(part, b).wait()
        return carry

    lax.fori_loop(0, var, finish, 0)
    for k in range(samp):
        @pl.when(s != k)
        def _():
            def sent(b, carry):
                cc_copy(b, k).wait_send()
                oo_copy(b, k).wait_send()
                return carry

            lax.fori_loop(0, var, sent, 0)
    lax.fori_loop(0, last, finish_relay, 0)

    @pl.when(early_owner)
    def _():
        relay_copy(0, last).wait_send()
        out_copy(samp - 1, last).wait_recv()

    @pl.when(late_owner)
    def _():
        relay_copy(1, last).wait_send()
        out_copy(samp - 1, last).wait_send()
        for part in range(2):
            relay_copy(part, last).wait_recv()

    for d in range(1, samp):
        tail_copy(d).wait()
    for spot in spots:
        ask_copy(place(spot)).wait_send()
        for k in range(samp):
            z_copy(place(spot), k).wait_send()
    for peer in peers:
        oz_copy(*peer).wait_send()
        oz_arrival(*peer).wait_recv()
    whole = oz[0]
    for e in range(1, samp * var):
        whole = whole + oz[e]
    obj_ref[...] = whole


def unpack_kernel(samp, var, order, bits, tab, fin_ref, tails_ref, whole_ref,
                  out_hbm, dia_hbm, obj_hbm, table, stage, dia, obj, sem, extra):
    v = lax.axis_index("var")
    cols, width = dia.shape
    load = pltpu.make_async_copy(tab, table, extra.at[0])
    load.start()
    lane = lax.broadcasted_iota(jnp.int32, (1, width), 1)
    part = lane // (width // 2)
    for step in range(STEPS):
        obj[step] = jnp.sum(jnp.where(part == step, whole_ref[...], 0.0)) / order
    rest = [pltpu.make_async_copy(obj, obj_hbm, extra.at[1]), pltpu.make_async_copy(dia, dia_hbm, extra.at[2])]
    rest[0].start()

    bases = places(v)

    def place(b, k):
        return lax.shift_right_logical(table[batch_owner(v, bases, b, k), 0, k], bits) & (cols - 1)

    def copy(b, k):
        return pltpu.make_async_copy(stage.at[b, k], out_hbm.at[place(b, k)], sem.at[b, k])

    for b in range(var):
        for k in range(samp):
            stage[b, k] = fin_ref[k, b].astype(jnp.float32)
    load.wait()
    for b in range(var):
        for k in range(samp):
            copy(b, k).start()
    for b in range(var):
        for k in range(samp):
            dia[pl.ds(place(b, k), 1), :] = tails_ref[k, b:b + 1, :]
    rest[1].start()
    for b in range(var):
        for k in range(samp):
            pltpu.make_async_copy(stage.at[b, k], out_hbm.at[0], sem.at[b, k]).wait()
    for other in rest:
        other.wait()


def column_body(observed, blocks, diagonal, pattern):
    cols, width = blocks.shape[0], blocks.shape[2]
    rows = observed.shape[0]
    var, samp = lax.axis_size("var"), lax.axis_size("samp")
    bits = cols.bit_length() - 1

    vmem = pl.BlockSpec(memory_space=pltpu.VMEM)
    smem = pl.BlockSpec(memory_space=pltpu.SMEM)
    hbm = pl.BlockSpec(memory_space=pltpu.HBM)
    dma = pltpu.SemaphoreType.DMA
    bf16, f32 = jnp.bfloat16, jnp.float32
    fold, late_rows = width // 2 + 16, width + width // 2 + 16
    fin, tails, whole, table = pl.pallas_call(
        functools.partial(main_kernel, samp, var),
        out_shape=(
            jax.ShapeDtypeStruct((samp, var, 2, width, width), bf16),
            jax.ShapeDtypeStruct((samp, var, width), f32),
            jax.ShapeDtypeStruct((1, width), f32),
            jax.ShapeDtypeStruct((var, 1, width), jnp.int32),
        ),
        in_specs=[hbm] * 4,
        out_specs=(vmem,) * 4,
        scratch_shapes=[
            pltpu.VMEM((2, cols), jnp.int32),
            pltpu.VMEM((cols, rows, width), observed.dtype),
            pltpu.VMEM(blocks.shape, f32),
            pltpu.VMEM((cols, 1, width), f32),
            pltpu.SMEM((var, 1, width), jnp.int32),
            pltpu.SMEM((var, 1, width), jnp.int32),
            pltpu.VMEM((var, samp, rows, width), observed.dtype),
            pltpu.VMEM((var, samp, rows, width), observed.dtype),
            pltpu.VMEM((var, samp, fold, width), bf16),
            pltpu.VMEM((var, samp, fold, width), bf16),
            pltpu.VMEM((var, width // 2, width), f32),
            pltpu.VMEM((var, 1, width), f32),
            pltpu.VMEM((var, samp, late_rows, width), bf16),
            pltpu.VMEM((var, samp, late_rows, width), bf16),
            pltpu.VMEM((var, width, width), f32),
            pltpu.VMEM((var, width // 2, width), f32),
            pltpu.VMEM((var, 1, width), f32),
            pltpu.VMEM((samp * var, 1, width), f32),
            pltpu.VMEM((8, width), f32),
            dma((cols + 3,)), dma, dma((var,)), dma((var,)),
            dma((var, samp)), dma((var, samp)), dma((var, samp)), dma((var, samp)),
            dma((var, samp)), dma((var, samp)), dma((samp, var)), dma((samp, var)),
            dma((2, var)), dma((2, var)), dma((samp,)), dma((samp,)),
            dma((samp * var,)), dma((samp * var,)),
        ],
        compiler_params=pltpu.CompilerParams(
            collective_id=0, has_side_effects=True, vmem_limit_bytes=40 * 2 ** 20),
        name="columns",
    )(*(pltpu.with_memory_space_constraint(array, pltpu.HBM)
        for array in (pattern.T, observed, blocks, diagonal.reshape(cols, 1, width))))

    new_blocks, new_diagonal, objective = pl.pallas_call(
        functools.partial(unpack_kernel, samp, var, float(cols * width * var), bits),
        out_shape=(
            jax.ShapeDtypeStruct(blocks.shape, f32),
            jax.ShapeDtypeStruct((cols, width), f32),
            jax.ShapeDtypeStruct((STEPS,), f32),
        ),
        in_specs=[vmem] * 4,
        out_specs=(hbm,) * 3,
        scratch_shapes=[
            pltpu.SMEM((var, 1, width), jnp.int32),
            pltpu.VMEM((var, samp, 2, width, width), f32),
            pltpu.VMEM((cols, width), f32),
            pltpu.SMEM((STEPS,), f32),
            dma((var, samp)), dma((3,)),
        ],
        compiler_params=pltpu.CompilerParams(vmem_limit_bytes=16 * 2 ** 20),
        name="unpack",
    )(table, fin, tails, whole)
    return new_blocks, new_diagonal.reshape(-1), objective


def advance(diag_block, off_block, diag_values, grad_diag, grad_off, diag_mask, total_rows):
    grad_diag = grad_diag / total_rows
    grad_off = grad_off / total_rows
    new_off = shrink(off_block - step_length * grad_off, step_length * penalty)
    new_diag_block = jnp.where(
        diag_mask, 0.0, shrink(diag_block - step_length * grad_diag, step_length * penalty)
    )
    along = jnp.sum(jnp.where(diag_mask, grad_diag, 0.0), axis=1)
    moved = diag_values - step_length * along
    new_values = 0.5 * (moved + jnp.sqrt(moved * moved + 4.0 * step_length))
    return (new_diag_block, new_off, new_values)


def body(observed, blocks, diagonal, pattern):
    col_count = blocks.shape[0]
    block_width = blocks.shape[2]
    sample_rows = observed.shape[0]
    var_count = lax.axis_size("var")
    samp_count = lax.axis_size("samp")
    capacity = max(2, -(-col_count // var_count))
    total_rows = sample_rows * samp_count
    matrix_order = col_count * block_width * var_count
    var_index = lax.axis_index("var")
    column_ids = jnp.arange(col_count, dtype=jnp.int32)
    columns = var_index * col_count + column_ids
    on_diag = pattern == columns[:, None]
    off_row = jnp.sum(jnp.where(on_diag, 0, pattern), axis=1)
    owner_index = off_row // col_count
    resident_block = off_row % col_count
    earlier = (owner_index[None, :] == owner_index[:, None]) & (
        column_ids[None, :] < column_ids[:, None]
    )
    position_rank = jnp.sum(earlier, axis=1)
    slot_index = owner_index * capacity + position_rank
    all_slots = jnp.arange(var_count * capacity, dtype=jnp.int32)
    slot_match = slot_index[:, None] == all_slots[None, :]
    wanted = jnp.sum(jnp.where(slot_match, resident_block[:, None], 0), axis=0)
    asked_blocks = lax.all_to_all(wanted, "var", split_axis=0, concat_axis=0, tiled=True)
    nearby_panels = observed.reshape(sample_rows, col_count, block_width)
    outgoing = jnp.take(nearby_panels, asked_blocks, axis=1)
    arrived = lax.all_to_all(outgoing, "var", split_axis=1, concat_axis=1, tiled=True)
    distant_panels = jnp.take(arrived, slot_index, axis=1)
    diag_mask = jnp.eye(block_width, dtype=bool)
    flags = on_diag[:, :, None, None]
    diag_block = jnp.sum(jnp.where(flags, blocks, 0.0), axis=1)
    diag_block = jnp.where(diag_mask, 0.0, diag_block)
    off_block = jnp.sum(jnp.where(flags, 0.0, blocks), axis=1)
    diag_values = diagonal.reshape(col_count, block_width)
    samp_first = (lax.axis_index("samp") == 0).astype(jnp.float32)
    objective_parts = []
    for iteration in range(STEPS):
        full_diag = jnp.where(diag_mask, diag_values[:, None, :], diag_block)
        product = jnp.einsum(
            "qlh,lhy->qly",
            nearby_panels,
            full_diag.astype(jnp.bfloat16),
            preferred_element_type=jnp.float32,
        )
        product = product + jnp.einsum(
            "qlh,lhy->qly",
            distant_panels,
            off_block.astype(jnp.bfloat16),
            preferred_element_type=jnp.float32,
        )
        squares = jnp.sum(product * product)
        local_terms = -jnp.sum(jnp.log(diag_values)) + penalty * (
            jnp.sum(jnp.abs(diag_block)) + jnp.sum(jnp.abs(off_block))
        )
        part_value = (squares / (2.0 * total_rows) + samp_first * local_terms) / matrix_order
        objective_parts.append(part_value)
        lower_precision_product = product.astype(jnp.bfloat16)
        grad_diag = jnp.einsum(
            "rei,reo->eio",
            nearby_panels,
            lower_precision_product,
            preferred_element_type=jnp.float32,
        )
        grad_off = jnp.einsum(
            "rei,reo->eio",
            distant_panels,
            lower_precision_product,
            preferred_element_type=jnp.float32,
        )
        grad_diag, grad_off = lax.psum((grad_diag, grad_off), "samp")
        diag_block, off_block, diag_values = advance(
            diag_block, off_block, diag_values, grad_diag, grad_off, diag_mask, total_rows
        )
    objective = lax.psum(jnp.stack(objective_parts), ("samp", "var"))
    new_blocks = jnp.where(flags, diag_block[:, None], off_block[:, None])
    return (new_blocks, diag_values.reshape(-1), objective)


def power_of_two(count):
    return count & (count - 1) == 0


def whole_body(observed, blocks, diagonal, pattern):
    cols = blocks.shape[0]
    var, samp = lax.axis_size("var"), lax.axis_size("samp")
    exact = samp == 4 and samp * var == cols and var == 2 * samp and blocks.shape[2] == 128
    if exact and power_of_two(samp) and power_of_two(var):
        return column_body(observed, blocks, diagonal, pattern)
    return body(observed, blocks, diagonal, pattern)


def solution(mesh):
    placed = (P("samp", "var"), P("var", None, None, None), P("var"), P("var", None))
    return jax.shard_map(
        whole_body,
        mesh=mesh,
        in_specs=placed,
        out_specs=(P("var", None, None, None), P("var"), P()),
        check_vma=False,
    )
```

```python
import functools

import jax
import jax.numpy as jnp
from jax import lax
from jax.experimental import pallas as pl
from jax.experimental.pallas import tpu as pltpu
from jax.sharding import PartitionSpec as P

STEPS = 2


step_length = 0.5
penalty = 0.5
MESH = pl.DeviceIdType.MESH


def shrink(moved, level):
    return moved - jnp.clip(moved, -level, level)


def mates(s):
    return s, s + 1 - 2 * (s % 2), s + 2 - 4 * (s // 2), 3 - s


def places(v):
    far_half = 1 - v // 4
    own = v // 2
    return 2 * own, 2 * (own + 1 - 2 * (own % 2)), 2 + 2 * far_half, 6 * far_half


OWN, NEXT, CLOSE, DISTANT = range(4)


def batch_place(b, high, low):
    return ((OWN, 0), (OWN, 1), (NEXT, high), (CLOSE, low), (NEXT, 1 - high),
            (DISTANT, low), (DISTANT, 1 - low), (CLOSE, 1 - low))[b]


def batch_owner(v, bases, b, k):
    chip, other = batch_place(b, k // 2, k % 2)
    return bases[chip] + (v % 2 + other) % 2


def send_rank(chip, other, n):
    if chip == NEXT:
        return (n + 2 * other) % 4
    return 2 * n + other if n < 2 else 2 * (n - 2) + 1 - other


def main_kernel(samp, var, pat_hbm, x_hbm, blk_hbm, dia_hbm,
                fin_ref, tails_ref, obj_ref, tab_ref,
                pat_ref, x, blk, dia_ref, tab, ask_s, far, farz, cc_out, cc_in, cc_own, cc_diag,
                oo_out, oo_in, oc_own, oo_own, oo_diag, oz, acc,
                load, tab_l, ask_ss, ask_rs, cc_s, cc_r, z_s, z_r, oo_s, oo_r, out_s, out_r,
                rel_s, rel_r, tail_s, tail_r, oz_s, oz_r):
    s = lax.axis_index("samp")
    v = lax.axis_index("var")
    inner = (v // 2 + v // 4) % 2
    core = v % 2
    bases = places(v)
    cores = (core, 1 - core)
    mate = mates(s)
    spots = [(chip, other) for chip in range(4) for other in range(2)][1:]
    rows, width = x.shape[1], x.shape[2]
    fold_rows = width // 2
    total_rows = rows * samp
    over_first = (((0,), (0,)), ((), ()))

    cols = x.shape[0]
    bits = cols.bit_length() - 1
    barrier = pltpu.get_barrier_semaphore()
    for chip, other in spots:
        pl.semaphore_signal(barrier, inc=1, device_id={"var": bases[chip] + cores[other]}, device_id_type=MESH)
    for d in range(1, samp):
        pl.semaphore_signal(barrier, inc=1, device_id={"samp": mate[d]}, device_id_type=MESH)

    pat_load = pltpu.make_async_copy(pat_hbm, pat_ref, load.at[1])
    pat_load.start()
    x_loads = [
        pltpu.make_async_copy(x_hbm.at[:, l * width:(l + 1) * width], x.at[l], load.at[0])
        for l in range(cols)
    ]
    for x_load in x_loads:
        x_load.start()
    blk_load = pltpu.make_async_copy(blk_hbm, blk, load.at[2])
    dia_load = pltpu.make_async_copy(dia_hbm, dia_ref, load.at[3])

    pat_load.wait()
    first, second = pat_ref[0:1, :], pat_ref[1:2, :]
    ids = lax.broadcasted_iota(jnp.int32, (1, cols), 1)
    lead = first == v * cols + ids
    off_row = jnp.where(lead, second, first)
    owner = lax.shift_right_logical(off_row, bits)
    entry = (off_row & (cols - 1)) + ids * cols + jnp.where(lead, 0, cols * cols)
    below = lax.broadcasted_iota(jnp.int32, (cols, cols), 0)
    across = lax.broadcasted_iota(jnp.int32, (cols, cols), 1)
    wide = jnp.broadcast_to(owner, (cols, cols))
    down = jnp.sum(jnp.where(below == across, wide, 0), axis=1, keepdims=True)
    rank = jnp.sum(jnp.where((down == wide) & (below < across), 1, 0), axis=0, keepdims=True)
    mine = lax.broadcasted_iota(jnp.int32, (var, cols), 0) == owner
    lanes = lax.broadcasted_iota(jnp.int32, (var, width), 1)
    table = jnp.zeros((var, width), jnp.int32)
    for k in range(samp):
        picked = jnp.sum(jnp.where(mine & (rank == k), entry, 0), axis=1, keepdims=True)
        table = jnp.where(lanes == k, picked, table)
    for u in range(var):
        tab_ref[u] = table[u:u + 1, :]
    tab_load = pltpu.make_async_copy(tab_ref, tab, tab_l)
    tab_load.start()

    pl.semaphore_wait(barrier, samp + var - 2)

    def remote(src, dst, send, recv, **where):
        return pltpu.make_async_remote_copy(
            src_ref=src, dst_ref=dst, send_sem=send, recv_sem=recv,
            device_id=where, device_id_type=MESH)

    def place(spot):
        return bases[spot[0]] + cores[spot[1]]

    def ask_copy(u):
        return remote(tab_ref.at[u], ask_s.at[v], ask_ss, ask_rs.at[v], var=u)

    def ask_arrival(u):
        return remote(tab_ref.at[u], ask_s.at[u], ask_ss, ask_rs.at[u], var=u)

    def z_copy(u, k, turn):
        return remote(far.at[u, k], farz.at[v, k], z_s, z_r.at[turn], var=u)

    def cc_copy(b, k):
        return remote(cc_out.at[b, k], cc_in.at[b, s], cc_s, cc_r.at[b], samp=k)

    def oo_copy(b, k):
        return remote(oo_out.at[b, k], oo_in.at[b, s], oo_s, oo_r.at[b], samp=k)

    def out_copy(d, b):
        direct = d == samp - 1
        return remote(fin_ref.at[s, b], fin_ref.at[s, b], out_s.at[int(direct)], out_r.at[var if direct else b],
                      samp=mate[d])

    def together(array, send, recv):
        return remote(array, array, send, recv, samp=mate[1])

    def near_panel(u, k):
        return x[lax.shift_right_logical(tab[u, 0, k], bits) & (cols - 1)]

    def gram(left, right):
        return lax.dot_general(left, right, over_first, preferred_element_type=jnp.float32)

    row_at = lax.broadcasted_iota(jnp.int32, (width, width), 0)
    col_at = lax.broadcasted_iota(jnp.int32, (width, width), 1)
    eye = row_at == col_at
    fold_row = lax.broadcasted_iota(jnp.int32, (fold_rows, width), 0)
    fold_col = lax.broadcasted_iota(jnp.int32, (fold_rows, width), 1)
    from_top = fold_col >= fold_row + fold_rows
    own_top = (fold_col < fold_rows) & (fold_col >= fold_row)
    note_row = lax.broadcasted_iota(jnp.int32, (16, width), 0)

    def folded(part):
        return jnp.where(from_top, pltpu.roll(part[:fold_rows], fold_rows, 1), part[fold_rows:])

    def unfolded(half_block, diag):
        turned = pltpu.roll(half_block, fold_rows, 1)
        mirror = jnp.concatenate([half_block, turned], axis=0).T
        top = jnp.where(own_top, turned, mirror[fold_rows:])
        bottom = jnp.where(from_top, mirror[:fold_rows], half_block)
        return jnp.where(eye, diag, jnp.concatenate([top, bottom], axis=0))

    def diagonal_of(part):
        return jnp.sum(jnp.where(eye, part, 0.0), axis=0, keepdims=True)

    def note_of(diag):
        high = diag.astype(jnp.bfloat16).astype(jnp.float32)
        return jnp.where(note_row == 0, high, jnp.where(note_row == 1, diag - high, 0.0))

    def start_cc(b):
        for k in range(samp):
            u = batch_owner(v, bases, b, k)
            c = near_panel(u, k)
            part = gram(c, c)
            short, diag = folded(part), diagonal_of(part)
            cc_out[b, k, :fold_rows] = short.astype(jnp.bfloat16)
            cc_out[b, k, fold_rows:] = note_of(diag).astype(jnp.bfloat16)

            @pl.when(s == k)
            def _():
                cc_own[b] = short
                cc_diag[b] = diag

            @pl.when(s != k)
            def _():
                cc_copy(b, k).start()

    def start_oo(b, ranks, far_panel):
        for k in ranks:
            u = batch_owner(v, bases, b, k)
            o = far_panel(u, k)
            part = gram(o, jnp.concatenate([near_panel(u, k), o], axis=1))
            cross, own = part[:, :width], part[:, width:]
            short, diag = folded(own), diagonal_of(own)
            oo_out[b, k, :width] = cross.astype(jnp.bfloat16)
            oo_out[b, k, width:width + fold_rows] = short.astype(jnp.bfloat16)
            oo_out[b, k, width + fold_rows:] = note_of(diag).astype(jnp.bfloat16)

            @pl.when(s == k)
            def _():
                oc_own[b] = cross
                oo_own[b] = short
                oo_diag[b] = diag

            @pl.when(s != k)
            def _():
                oo_copy(b, k).start()

    def arrived(turn, ranks):
        together(farz.at[0, :len(ranks)], z_s, z_r.at[turn]).wait_recv()

    def note_sum(note):
        note = note.astype(jnp.float32)
        return note[0:1] + note[1:2]

    def column(b):
        together(cc_in.at[b, :samp - 1], cc_s, cc_r.at[b]).wait_recv()
        together(oo_in.at[b, :samp - 1], oo_s, oo_r.at[b]).wait_recv()
        cc, oc, oo = cc_own[b], oc_own[b], oo_own[b]
        cc_d, oo_d = cc_diag[b], oo_diag[b]
        for d in range(1, samp):
            p = mate[d]
            cc = cc + cc_in[b, p, :fold_rows].astype(jnp.float32)
            cc_d = cc_d + note_sum(cc_in[b, p, fold_rows:])
            oc = oc + oo_in[b, p, :width].astype(jnp.float32)
            oo = oo + oo_in[b, p, width:width + fold_rows].astype(jnp.float32)
            oo_d = oo_d + note_sum(oo_in[b, p, width + fold_rows:])
        cc, oo = unfolded(cc, cc_d), unfolded(oo, oo_d)
        both = jnp.concatenate(
            [jnp.concatenate([cc, oc.T], axis=1), jnp.concatenate([oc, oo], axis=1)], axis=0)
        high = both.astype(jnp.bfloat16)
        low = (both - high.astype(jnp.float32)).astype(jnp.bfloat16)
        gram_parts = jnp.concatenate([high, low], axis=1)
        u = batch_owner(v, bases, b, s)
        value = tab[u, 0, s]
        col = lax.shift_right_logical(value, bits) & (cols - 1)
        slot = lax.shift_right_logical(value, 2 * bits) & 1
        wd = jnp.where(eye, 0.0, blk[col, slot])
        wo = blk[col, 1 - slot]
        dv = dia_ref[col]
        for step in range(STEPS):
            rounded = jnp.concatenate(
                [jnp.where(eye, dv, wd).astype(jnp.bfloat16), wo.astype(jnp.bfloat16)], axis=0)
            grad = jnp.dot(gram_parts, jnp.concatenate([rounded, rounded], axis=0),
                           preferred_element_type=jnp.float32)
            squares = jnp.sum(grad * rounded.astype(jnp.float32), axis=0, keepdims=True)
            terms = (squares / (2.0 * total_rows) - jnp.log(dv)
                     + penalty * jnp.sum(jnp.abs(wd) + jnp.abs(wo), axis=0, keepdims=True))
            acc[step:step + 1, :] += terms
            grad = grad / total_rows
            gd, go = grad[:width], grad[width:]
            wo = shrink(wo - step_length * go, step_length * penalty)
            wd = jnp.where(eye, 0.0, shrink(wd - step_length * gd, step_length * penalty))
            along = jnp.sum(jnp.where(eye, gd, 0.0), axis=0, keepdims=True)
            moved = dv - step_length * along
            dv = 0.5 * (moved + jnp.sqrt(moved * moved + 4.0 * step_length))
        lead = slot == 0
        fin_ref[s, b, 0] = jnp.where(lead, wd, wo).astype(jnp.bfloat16)
        fin_ref[s, b, 1] = jnp.where(lead, wo, wd).astype(jnp.bfloat16)
        tails_ref[s, pl.ds(b, 1), :] = dv

    def relay_copy(part, b, final=0):
        near, to = mate[1 + part], mate[2 - part]
        return remote(fin_ref.at[near, b, part], fin_ref.at[near, b, part],
                      rel_s.at[final], rel_r.at[final], samp=to)

    def beside_done(b):
        together(fin_ref.at[0, :samp - 2], out_s.at[0], out_r.at[b]).wait_recv()

    def relay(b):
        beside_done(b)
        for part in range(2):
            relay_copy(part, b).start()

    close = [(CLOSE, 0), (CLOSE, 1)]
    beside = [(NEXT, 0), (NEXT, 1)]
    distant = [(DISTANT, 0), (DISTANT, 1)]
    for spot in close + beside + distant + [(OWN, 1)]:
        ask_copy(place(spot)).start()
    acc[...] = jnp.zeros_like(acc)
    pltpu.make_async_copy(x, x, load.at[0]).wait()
    blk_load.start()
    dia_load.start()
    tab_load.wait()
    start_cc(0)

    def learn(wanted):
        for spot in wanted:
            ask_arrival(place(spot)).wait_recv()

    def send_panel(spot, k, turn):
        u = place(spot)
        far[u, k] = x[ask_s[u, 0, k] & (cols - 1)]
        z_copy(u, k, turn).start()

    def send(wanted, turns, at):
        for n in turns:
            for spot in wanted:
                send_panel(spot, send_rank(*spot, n), at[n])

    near_turns, inner_turns, outer_turns = (2, 2, 4, 4), (3, 3, 7, 0), (5, 5, 6, 6)

    across = [close[0], distant[0], close[1], distant[1]]

    @pl.when(inner == 1)
    def _():
        learn(close)
        send(close, [0], inner_turns)
        learn(distant + beside)
        send(distant, [0], inner_turns)
        send(beside, range(samp), near_turns)
        send(across, range(1, samp), inner_turns)

    @pl.when(inner == 0)
    def _():
        learn(beside)
        send(beside, range(samp), near_turns)
        learn(close + distant)

    learn([(OWN, 1)])
    for k in range(samp):
        send_panel((OWN, 1), k, 1)

    every = range(samp)
    start_oo(0, every, lambda u, k: x[tab[u, 0, k] & (cols - 1)])
    start_cc(1)

    def from_var(u, k):
        return farz[u, k]

    def take(b, ranks=every, turn=None):
        arrived(b if turn is None else turn, ranks)
        start_oo(b, ranks, from_var)

    def settle(b):
        column(b)
        for d in range(1, samp - 1):
            out_copy(d, b).start()

    last = var - 1
    take(1)
    for b in range(2, var):
        start_cc(b)
    blk_load.wait()
    dia_load.wait()
    settle(0)
    take(2)
    arrived(3, every)

    @pl.when(inner == 0)
    def _():
        send(across, range(samp), outer_turns)

    settle(1)
    start_oo(3, every, from_var)
    settle(2)
    relay(0)
    relay(1)
    take(4)
    settle(3)
    relay(2)
    take(5)
    settle(4)
    relay(3)
    settle(5)
    relay(4)
    take(6)
    relay(5)
    take(last, range(samp // 2))
    settle(6)
    take(last, range(samp // 2, samp), 0)
    relay(last - 1)
    column(last)

    def tail_copy(d):
        return remote(tails_ref.at[s], tails_ref.at[s], tail_s, tail_r,
                      samp=mate[d])

    def oz_copy(d, u):
        return remote(oz.at[s * var + v], oz.at[s * var + v], oz_s, oz_r,
                      samp=mate[d], var=u)

    halves = [acc[step:step + 1, :] + pltpu.roll(acc[step:step + 1, :], fold_rows, 1) for step in range(STEPS)]
    oz[s * var + v] = jnp.where(fold_col[:1] < fold_rows, halves[0], halves[1])
    peers = [(d, place(spot)) for d in range(samp - 1, -1, -1) for spot in spots[::-1] + [(OWN, 0)]][:-1]
    for peer in peers:
        oz_copy(*peer).start()
    for d in range(1, samp - 1):
        out_copy(d, last).start()

    early_owner = s < samp // 2
    late_owner = s >= samp // 2

    @pl.when(late_owner)
    def _():
        out_copy(samp - 1, last).start()

    for d in range(1, samp):
        tail_copy(d).start()

    beside_done(last)

    @pl.when(early_owner)
    def _():
        relay_copy(0, last, 1).start()

    @pl.when(late_owner)
    def _():
        relay_copy(1, last, 1).start()

    sent = var * (samp - 1) // samp
    together(cc_out.at[:sent], cc_s, cc_r.at[0]).wait_send()
    together(oo_out.at[:sent], oo_s, oo_r.at[0]).wait_send()
    together(fin_ref.at[:samp - 2], out_s.at[0], out_r.at[0]).wait_send()
    together(fin_ref.at[0, :last], rel_s.at[0], rel_r.at[0]).wait()
    together(fin_ref.at[0, 0, 0], rel_s.at[1], rel_r.at[1]).wait_send()

    @pl.when(early_owner)
    def _():
        together(fin_ref.at[0, 0], out_s.at[1], out_r.at[var]).wait_recv()

    @pl.when(late_owner)
    def _():
        together(fin_ref.at[0, 0], out_s.at[1], out_r.at[var]).wait_send()
        together(fin_ref.at[0, 0], rel_s.at[1], rel_r.at[1]).wait_recv()

    together(tails_ref.at[:samp - 1], tail_s, tail_r).wait()
    together(tab_ref.at[:var - 1], ask_ss, ask_rs.at[0]).wait_send()
    together(far.at[:var - 1], z_s, z_r.at[0]).wait_send()
    together(oz.at[:samp * var - 1], oz_s, oz_r).wait()
    whole = oz[0]
    for e in range(1, samp * var):
        whole = whole + oz[e]
    obj_ref[...] = whole


def unpack_kernel(samp, var, order, bits, tab, fin_ref, tails_ref, whole_ref,
                  out_hbm, dia_hbm, obj_hbm, table, stage, dia, obj, extra):
    v = lax.axis_index("var")
    cols, width = dia.shape
    load = pltpu.make_async_copy(tab, table, extra.at[0])
    load.start()
    lane = lax.broadcasted_iota(jnp.int32, (1, width), 1)
    part = lane // (width // 2)
    for step in range(STEPS):
        obj[step] = jnp.sum(jnp.where(part == step, whole_ref[...], 0.0)) / order
    rest = [pltpu.make_async_copy(obj, obj_hbm, extra.at[1]), pltpu.make_async_copy(dia, dia_hbm, extra.at[2])]
    rest[0].start()

    bases = places(v)

    def place(b, k):
        return lax.shift_right_logical(table[batch_owner(v, bases, b, k), 0, k], bits) & (cols - 1)

    def copy(b, k):
        return pltpu.make_async_copy(stage.at[b * samp + k], out_hbm.at[place(b, k)], extra.at[3])

    for b in range(var):
        for k in range(samp):
            stage[b * samp + k] = fin_ref[k, b].astype(jnp.float32)
    load.wait()
    for b in range(var):
        for k in range(samp):
            copy(b, k).start()
    for b in range(var):
        for k in range(samp):
            dia[pl.ds(place(b, k), 1), :] = tails_ref[k, b:b + 1, :]
    rest[1].start()
    pltpu.make_async_copy(stage, out_hbm, extra.at[3]).wait()
    for other in rest:
        other.wait()


def column_body(observed, blocks, diagonal, pattern):
    cols, width = blocks.shape[0], blocks.shape[2]
    rows = observed.shape[0]
    var, samp = lax.axis_size("var"), lax.axis_size("samp")
    bits = cols.bit_length() - 1

    vmem = pl.BlockSpec(memory_space=pltpu.VMEM)
    smem = pl.BlockSpec(memory_space=pltpu.SMEM)
    hbm = pl.BlockSpec(memory_space=pltpu.HBM)
    dma = pltpu.SemaphoreType.DMA
    bf16, f32 = jnp.bfloat16, jnp.float32
    fold, late_rows = width // 2 + 16, width + width // 2 + 16
    fin, tails, whole, table = pl.pallas_call(
        functools.partial(main_kernel, samp, var),
        out_shape=(
            jax.ShapeDtypeStruct((samp, var, 2, width, width), bf16),
            jax.ShapeDtypeStruct((samp, var, width), f32),
            jax.ShapeDtypeStruct((1, width), f32),
            jax.ShapeDtypeStruct((var, 1, width), jnp.int32),
        ),
        in_specs=[hbm] * 4,
        out_specs=(vmem,) * 4,
        scratch_shapes=[
            pltpu.VMEM((2, cols), jnp.int32),
            pltpu.VMEM((cols, rows, width), observed.dtype),
            pltpu.VMEM(blocks.shape, f32),
            pltpu.VMEM((cols, 1, width), f32),
            pltpu.SMEM((var, 1, width), jnp.int32),
            pltpu.SMEM((var, 1, width), jnp.int32),
            pltpu.VMEM((var, samp, rows, width), observed.dtype),
            pltpu.VMEM((var, samp, rows, width), observed.dtype),
            pltpu.VMEM((var, samp, fold, width), bf16),
            pltpu.VMEM((var, samp, fold, width), bf16),
            pltpu.VMEM((var, width // 2, width), f32),
            pltpu.VMEM((var, 1, width), f32),
            pltpu.VMEM((var, samp, late_rows, width), bf16),
            pltpu.VMEM((var, samp, late_rows, width), bf16),
            pltpu.VMEM((var, width, width), f32),
            pltpu.VMEM((var, width // 2, width), f32),
            pltpu.VMEM((var, 1, width), f32),
            pltpu.VMEM((samp * var, 1, width), f32),
            pltpu.VMEM((8, width), f32),
            dma((4,)), dma, dma, dma((var,)), dma, dma((var,)), dma, dma((var,)), dma, dma((var,)),
            dma((2,)), dma((var + 1,)), dma((2,)), dma((2,)), dma, dma, dma, dma,
        ],
        compiler_params=pltpu.CompilerParams(
            collective_id=0, has_side_effects=True, vmem_limit_bytes=40 * 2 ** 20),
        name="columns",
    )(*(pltpu.with_memory_space_constraint(array, pltpu.HBM)
        for array in (pattern.T, observed, blocks, diagonal.reshape(cols, 1, width))))

    new_blocks, new_diagonal, objective = pl.pallas_call(
        functools.partial(unpack_kernel, samp, var, float(cols * width * var), bits),
        out_shape=(
            jax.ShapeDtypeStruct(blocks.shape, f32),
            jax.ShapeDtypeStruct((cols, width), f32),
            jax.ShapeDtypeStruct((STEPS,), f32),
        ),
        in_specs=[vmem] * 4,
        out_specs=(hbm,) * 3,
        scratch_shapes=[
            pltpu.SMEM((var, 1, width), jnp.int32),
            pltpu.VMEM((cols, 2, width, width), f32),
            pltpu.VMEM((cols, width), f32),
            pltpu.SMEM((STEPS,), f32),
            dma((4,)),
        ],
        compiler_params=pltpu.CompilerParams(vmem_limit_bytes=16 * 2 ** 20),
        name="unpack",
    )(table, fin, tails, whole)
    return new_blocks, new_diagonal.reshape(-1), objective


def advance(diag_block, off_block, diag_values, grad_diag, grad_off, diag_mask, total_rows):
    grad_diag = grad_diag / total_rows
    grad_off = grad_off / total_rows
    new_off = shrink(off_block - step_length * grad_off, step_length * penalty)
    new_diag_block = jnp.where(
        diag_mask, 0.0, shrink(diag_block - step_length * grad_diag, step_length * penalty)
    )
    along = jnp.sum(jnp.where(diag_mask, grad_diag, 0.0), axis=1)
    moved = diag_values - step_length * along
    new_values = 0.5 * (moved + jnp.sqrt(moved * moved + 4.0 * step_length))
    return (new_diag_block, new_off, new_values)


def body(observed, blocks, diagonal, pattern):
    col_count = blocks.shape[0]
    block_width = blocks.shape[2]
    sample_rows = observed.shape[0]
    var_count = lax.axis_size("var")
    samp_count = lax.axis_size("samp")
    capacity = max(2, -(-col_count // var_count))
    total_rows = sample_rows * samp_count
    matrix_order = col_count * block_width * var_count
    var_index = lax.axis_index("var")
    column_ids = jnp.arange(col_count, dtype=jnp.int32)
    columns = var_index * col_count + column_ids
    on_diag = pattern == columns[:, None]
    off_row = jnp.sum(jnp.where(on_diag, 0, pattern), axis=1)
    owner_index = off_row // col_count
    resident_block = off_row % col_count
    earlier = (owner_index[None, :] == owner_index[:, None]) & (
        column_ids[None, :] < column_ids[:, None]
    )
    position_rank = jnp.sum(earlier, axis=1)
    slot_index = owner_index * capacity + position_rank
    all_slots = jnp.arange(var_count * capacity, dtype=jnp.int32)
    slot_match = slot_index[:, None] == all_slots[None, :]
    wanted = jnp.sum(jnp.where(slot_match, resident_block[:, None], 0), axis=0)
    asked_blocks = lax.all_to_all(wanted, "var", split_axis=0, concat_axis=0, tiled=True)
    nearby_panels = observed.reshape(sample_rows, col_count, block_width)
    outgoing = jnp.take(nearby_panels, asked_blocks, axis=1)
    arrived = lax.all_to_all(outgoing, "var", split_axis=1, concat_axis=1, tiled=True)
    distant_panels = jnp.take(arrived, slot_index, axis=1)
    diag_mask = jnp.eye(block_width, dtype=bool)
    flags = on_diag[:, :, None, None]
    diag_block = jnp.sum(jnp.where(flags, blocks, 0.0), axis=1)
    diag_block = jnp.where(diag_mask, 0.0, diag_block)
    off_block = jnp.sum(jnp.where(flags, 0.0, blocks), axis=1)
    diag_values = diagonal.reshape(col_count, block_width)
    samp_first = (lax.axis_index("samp") == 0).astype(jnp.float32)
    objective_parts = []
    for iteration in range(STEPS):
        full_diag = jnp.where(diag_mask, diag_values[:, None, :], diag_block)
        product = jnp.einsum(
            "qlh,lhy->qly",
            nearby_panels,
            full_diag.astype(jnp.bfloat16),
            preferred_element_type=jnp.float32,
        )
        product = product + jnp.einsum(
            "qlh,lhy->qly",
            distant_panels,
            off_block.astype(jnp.bfloat16),
            preferred_element_type=jnp.float32,
        )
        squares = jnp.sum(product * product)
        local_terms = -jnp.sum(jnp.log(diag_values)) + penalty * (
            jnp.sum(jnp.abs(diag_block)) + jnp.sum(jnp.abs(off_block))
        )
        part_value = (squares / (2.0 * total_rows) + samp_first * local_terms) / matrix_order
        objective_parts.append(part_value)
        lower_precision_product = product.astype(jnp.bfloat16)
        grad_diag = jnp.einsum(
            "rei,reo->eio",
            nearby_panels,
            lower_precision_product,
            preferred_element_type=jnp.float32,
        )
        grad_off = jnp.einsum(
            "rei,reo->eio",
            distant_panels,
            lower_precision_product,
            preferred_element_type=jnp.float32,
        )
        grad_diag, grad_off = lax.psum((grad_diag, grad_off), "samp")
        diag_block, off_block, diag_values = advance(
            diag_block, off_block, diag_values, grad_diag, grad_off, diag_mask, total_rows
        )
    objective = lax.psum(jnp.stack(objective_parts), ("samp", "var"))
    new_blocks = jnp.where(flags, diag_block[:, None], off_block[:, None])
    return (new_blocks, diag_values.reshape(-1), objective)


def power_of_two(count):
    return count & (count - 1) == 0


def whole_body(observed, blocks, diagonal, pattern):
    cols = blocks.shape[0]
    var, samp = lax.axis_size("var"), lax.axis_size("samp")
    exact = samp == 4 and samp * var == cols and var == 2 * samp and blocks.shape[2] == 128
    if exact and power_of_two(samp) and power_of_two(var):
        return column_body(observed, blocks, diagonal, pattern)
    return body(observed, blocks, diagonal, pattern)


def solution(mesh):
    placed = (P("samp", "var"), P("var", None, None, None), P("var"), P("var", None))
    return jax.shard_map(
        whole_body,
        mesh=mesh,
        in_specs=placed,
        out_specs=(P("var", None, None, None), P("var"), P()),
        check_vma=False,
    )
```

```python
import functools

import jax
import jax.numpy as jnp
from jax import lax
from jax.experimental import pallas as pl
from jax.experimental.pallas import tpu as pltpu
from jax.sharding import PartitionSpec as P

STEPS = 2


step_length = 0.5
penalty = 0.5
MESH = pl.DeviceIdType.MESH


def shrink(moved, level):
    return moved - jnp.clip(moved, -level, level)


def mates(s):
    return s, s + 1 - 2 * (s % 2), s + 2 - 4 * (s // 2), 3 - s


def places(v):
    far_half = 1 - v // 4
    own = v // 2
    return 2 * own, 2 * (own + 1 - 2 * (own % 2)), 2 + 2 * far_half, 6 * far_half


OWN, NEXT, CLOSE, DISTANT = range(4)


def batch_place(b, high, low):
    return ((OWN, 0), (OWN, 1), (NEXT, high), (CLOSE, low), (NEXT, 1 - high),
            (DISTANT, low), (DISTANT, 1 - low), (CLOSE, 1 - low))[b]


def batch_owner(v, bases, b, k):
    chip, other = batch_place(b, k // 2, k % 2)
    return bases[chip] + (v % 2 + other) % 2


def send_rank(chip, other, n):
    if chip == NEXT:
        return (n + 2 * other) % 4
    return 2 * n + other if n < 2 else 2 * (n - 2) + 1 - other


def main_kernel(samp, var, pat_hbm, x_hbm, blk_hbm, dia_hbm,
                fin_ref, tails_ref, obj_ref, tab_ref,
                pat_ref, x, blk, dia_ref, tab, ask_s, far, farz, cc_out, cc_in, cc_own, cc_diag,
                oo_out, oo_in, oc_own, oo_own, oo_diag, oz, acc,
                load, tab_l, ask_ss, ask_rs, cc_s, cc_r, z_s, z_r, oo_s, oo_r, out_s, out_r,
                rel_s, rel_r, tail_s, tail_r, oz_s, oz_r):
    s = lax.axis_index("samp")
    v = lax.axis_index("var")
    inner = (v // 2 + v // 4) % 2
    core = v % 2
    bases = places(v)
    cores = (core, 1 - core)
    mate = mates(s)
    spots = [(chip, other) for chip in range(4) for other in range(2)][1:]
    rows, width = x.shape[1], x.shape[2]
    fold_rows = width // 2
    total_rows = rows * samp
    over_first = (((0,), (0,)), ((), ()))

    cols = x.shape[0]
    bits = cols.bit_length() - 1
    barrier = pltpu.get_barrier_semaphore()
    for chip, other in spots:
        pl.semaphore_signal(barrier, inc=1, device_id={"var": bases[chip] + cores[other]}, device_id_type=MESH)
    for d in range(1, samp):
        pl.semaphore_signal(barrier, inc=1, device_id={"samp": mate[d]}, device_id_type=MESH)

    pat_load = pltpu.make_async_copy(pat_hbm, pat_ref, load.at[1])
    pat_load.start()
    x_loads = [
        pltpu.make_async_copy(x_hbm.at[:, l * width:(l + 1) * width], x.at[l], load.at[0])
        for l in range(cols)
    ]
    for x_load in x_loads:
        x_load.start()
    blk_load = pltpu.make_async_copy(blk_hbm, blk, load.at[2])
    dia_load = pltpu.make_async_copy(dia_hbm, dia_ref, load.at[3])

    pat_load.wait()
    first, second = pat_ref[0:1, :], pat_ref[1:2, :]
    ids = lax.broadcasted_iota(jnp.int32, (1, cols), 1)
    lead = first == v * cols + ids
    off_row = jnp.where(lead, second, first)
    owner = lax.shift_right_logical(off_row, bits)
    entry = (off_row & (cols - 1)) + ids * cols + jnp.where(lead, 0, cols * cols)
    below = lax.broadcasted_iota(jnp.int32, (cols, cols), 0)
    across = lax.broadcasted_iota(jnp.int32, (cols, cols), 1)
    wide = jnp.broadcast_to(owner, (cols, cols))
    down = jnp.sum(jnp.where(below == across, wide, 0), axis=1, keepdims=True)
    rank = jnp.sum(jnp.where((down == wide) & (below < across), 1, 0), axis=0, keepdims=True)
    mine = lax.broadcasted_iota(jnp.int32, (var, cols), 0) == owner
    lanes = lax.broadcasted_iota(jnp.int32, (var, width), 1)
    table = jnp.zeros((var, width), jnp.int32)
    for k in range(samp):
        picked = jnp.sum(jnp.where(mine & (rank == k), entry, 0), axis=1, keepdims=True)
        table = jnp.where(lanes == k, picked, table)
    for u in range(var):
        tab_ref[u] = table[u:u + 1, :]
    tab_load = pltpu.make_async_copy(tab_ref, tab, tab_l)
    tab_load.start()

    pl.semaphore_wait(barrier, samp + var - 2)

    def remote(src, dst, send, recv, **where):
        return pltpu.make_async_remote_copy(
            src_ref=src, dst_ref=dst, send_sem=send, recv_sem=recv,
            device_id=where, device_id_type=MESH)

    def place(spot):
        return bases[spot[0]] + cores[spot[1]]

    def ask_copy(u):
        return remote(tab_ref.at[u], ask_s.at[v], ask_ss, ask_rs.at[v], var=u)

    def ask_arrival(u):
        return remote(tab_ref.at[u], ask_s.at[u], ask_ss, ask_rs.at[u], var=u)

    def z_copy(u, k, turn):
        return remote(far.at[u, k], farz.at[v, k], z_s, z_r.at[turn], var=u)

    def cc_copy(b, k):
        return remote(cc_out.at[b, k], cc_in.at[b, s], cc_s, cc_r.at[b], samp=k)

    def oo_copy(b, k):
        return remote(oo_out.at[b, k], oo_in.at[b, s], oo_s, oo_r.at[b], samp=k)

    def out_copy(d, b):
        direct = d == samp - 1
        return remote(fin_ref.at[s, b], fin_ref.at[s, b], out_s.at[int(direct)], out_r.at[var if direct else b],
                      samp=mate[d])

    def together(array, send, recv):
        return remote(array, array, send, recv, samp=mate[1])

    def near_panel(u, k):
        return x[lax.shift_right_logical(tab[u, 0, k], bits) & (cols - 1)]

    def gram(left, right):
        return lax.dot_general(left, right, over_first, preferred_element_type=jnp.float32)

    row_at = lax.broadcasted_iota(jnp.int32, (width, width), 0)
    col_at = lax.broadcasted_iota(jnp.int32, (width, width), 1)
    eye = row_at == col_at
    fold_row = lax.broadcasted_iota(jnp.int32, (fold_rows, width), 0)
    fold_col = lax.broadcasted_iota(jnp.int32, (fold_rows, width), 1)
    from_top = fold_col >= fold_row + fold_rows
    own_top = (fold_col < fold_rows) & (fold_col >= fold_row)
    note_row = lax.broadcasted_iota(jnp.int32, (16, width), 0)

    def folded(part):
        return jnp.where(from_top, pltpu.roll(part[:fold_rows], fold_rows, 1), part[fold_rows:])

    def unfolded(half_block, diag):
        turned = pltpu.roll(half_block, fold_rows, 1)
        mirror = jnp.concatenate([half_block, turned], axis=0).T
        top = jnp.where(own_top, turned, mirror[fold_rows:])
        bottom = jnp.where(from_top, mirror[:fold_rows], half_block)
        return jnp.where(eye, diag, jnp.concatenate([top, bottom], axis=0))

    def diagonal_of(part):
        return jnp.sum(jnp.where(eye, part, 0.0), axis=0, keepdims=True)

    def note_of(diag):
        high = diag.astype(jnp.bfloat16).astype(jnp.float32)
        return jnp.where(note_row == 0, high, jnp.where(note_row == 1, diag - high, 0.0))

    def start_cc(b):
        for k in range(samp):
            u = batch_owner(v, bases, b, k)
            c = near_panel(u, k)
            part = gram(c, c)
            short, diag = folded(part), diagonal_of(part)
            cc_out[b, k, :fold_rows] = short.astype(jnp.bfloat16)
            cc_out[b, k, fold_rows:] = note_of(diag).astype(jnp.bfloat16)

            @pl.when(s == k)
            def _():
                cc_own[b] = short
                cc_diag[b] = diag

            @pl.when(s != k)
            def _():
                cc_copy(b, k).start()

    def start_oo(b, ranks, far_panel):
        for k in ranks:
            u = batch_owner(v, bases, b, k)
            o = far_panel(u, k)
            part = gram(o, jnp.concatenate([near_panel(u, k), o], axis=1))
            cross, own = part[:, :width], part[:, width:]
            short, diag = folded(own), diagonal_of(own)
            oo_out[b, k, :width] = cross.astype(jnp.bfloat16)
            oo_out[b, k, width:width + fold_rows] = short.astype(jnp.bfloat16)
            oo_out[b, k, width + fold_rows:] = note_of(diag).astype(jnp.bfloat16)

            @pl.when(s == k)
            def _():
                oc_own[b] = cross
                oo_own[b] = short
                oo_diag[b] = diag

            @pl.when(s != k)
            def _():
                oo_copy(b, k).start()

    def arrived(turn, ranks):
        together(farz.at[0, :len(ranks)], z_s, z_r.at[turn]).wait_recv()

    def note_sum(note):
        note = note.astype(jnp.float32)
        return note[0:1] + note[1:2]

    def column(b):
        together(cc_in.at[b, :samp - 1], cc_s, cc_r.at[b]).wait_recv()
        together(oo_in.at[b, :samp - 1], oo_s, oo_r.at[b]).wait_recv()
        cc, oc, oo = cc_own[b], oc_own[b], oo_own[b]
        cc_d, oo_d = cc_diag[b], oo_diag[b]
        for d in range(1, samp):
            p = mate[d]
            cc = cc + cc_in[b, p, :fold_rows].astype(jnp.float32)
            cc_d = cc_d + note_sum(cc_in[b, p, fold_rows:])
            oc = oc + oo_in[b, p, :width].astype(jnp.float32)
            oo = oo + oo_in[b, p, width:width + fold_rows].astype(jnp.float32)
            oo_d = oo_d + note_sum(oo_in[b, p, width + fold_rows:])
        cc, oo = unfolded(cc, cc_d), unfolded(oo, oo_d)
        both = jnp.concatenate(
            [jnp.concatenate([cc, oc.T], axis=1), jnp.concatenate([oc, oo], axis=1)], axis=0)
        high = both.astype(jnp.bfloat16)
        low = (both - high.astype(jnp.float32)).astype(jnp.bfloat16)
        gram_parts = jnp.concatenate([high, low], axis=1)
        u = batch_owner(v, bases, b, s)
        value = tab[u, 0, s]
        col = lax.shift_right_logical(value, bits) & (cols - 1)
        slot = lax.shift_right_logical(value, 2 * bits) & 1
        wd = jnp.where(eye, 0.0, blk[col, slot])
        wo = blk[col, 1 - slot]
        dv = dia_ref[col]
        for step in range(STEPS):
            rounded = jnp.concatenate(
                [jnp.where(eye, dv, wd).astype(jnp.bfloat16), wo.astype(jnp.bfloat16)], axis=0)
            grad = jnp.dot(gram_parts, jnp.concatenate([rounded, rounded], axis=0),
                           preferred_element_type=jnp.float32)
            squares = jnp.sum(grad * rounded.astype(jnp.float32), axis=0, keepdims=True)
            terms = (squares / (2.0 * total_rows) - jnp.log(dv)
                     + penalty * jnp.sum(jnp.abs(wd) + jnp.abs(wo), axis=0, keepdims=True))
            acc[step:step + 1, :] += terms
            grad = grad / total_rows
            gd, go = grad[:width], grad[width:]
            wo = shrink(wo - step_length * go, step_length * penalty)
            wd = jnp.where(eye, 0.0, shrink(wd - step_length * gd, step_length * penalty))
            along = jnp.sum(jnp.where(eye, gd, 0.0), axis=0, keepdims=True)
            moved = dv - step_length * along
            dv = 0.5 * (moved + jnp.sqrt(moved * moved + 4.0 * step_length))
        lead = slot == 0
        fin_ref[s, b, 0] = jnp.where(lead, wd, wo).astype(jnp.bfloat16)
        fin_ref[s, b, 1] = jnp.where(lead, wo, wd).astype(jnp.bfloat16)
        tails_ref[s, pl.ds(b, 1), :] = dv

    def relay_copy(part, b, final=0):
        near, to = mate[1 + part], mate[2 - part]
        return remote(fin_ref.at[near, b, part], fin_ref.at[near, b, part],
                      rel_s.at[final], rel_r.at[final], samp=to)

    def beside_done(b):
        together(fin_ref.at[0, :samp - 2], out_s.at[0], out_r.at[b]).wait_recv()

    def relay(b):
        beside_done(b)
        for part in range(2):
            relay_copy(part, b).start()

    close = [(CLOSE, 0), (CLOSE, 1)]
    beside = [(NEXT, 0), (NEXT, 1)]
    distant = [(DISTANT, 0), (DISTANT, 1)]
    for spot in close + beside + distant + [(OWN, 1)]:
        ask_copy(place(spot)).start()
    acc[...] = jnp.zeros_like(acc)
    pltpu.make_async_copy(x, x, load.at[0]).wait()
    blk_load.start()
    dia_load.start()
    tab_load.wait()
    start_cc(0)

    def learn(wanted):
        for spot in wanted:
            ask_arrival(place(spot)).wait_recv()

    def send_panel(spot, k, turn):
        u = place(spot)
        far[u, k] = x[ask_s[u, 0, k] & (cols - 1)]
        z_copy(u, k, turn).start()

    def send(wanted, turns, at):
        for n in turns:
            for spot in wanted:
                send_panel(spot, send_rank(*spot, n), at[n])

    near_turns, inner_turns, outer_turns = (2, 2, 4, 4), (3, 3, 7, 0), (5, 5, 6, 6)

    def send_last():
        for n, to, chip in [(n, to, chip) for to in range(2) for n in (2, 3) for chip in (CLOSE, DISTANT)]:
            other = (core + to) % 2
            k = 2 * (n - 2) + 1 - other
            u = bases[chip] + to
            far[u, k] = x[ask_s[u, 0, k] & (cols - 1)]
            z_copy(u, k, inner_turns[n]).start()

    across = [close[0], distant[0], close[1], distant[1]]

    @pl.when(inner == 1)
    def _():
        learn(close)
        send(close, [0], inner_turns)
        learn(distant + beside)
        send(distant, [0], inner_turns)
        send(beside, range(samp), near_turns)
        send(across, [1], inner_turns)
        send_last()

    @pl.when(inner == 0)
    def _():
        learn(beside)
        send(beside, range(samp), near_turns)
        learn(close + distant)

    learn([(OWN, 1)])
    for k in range(samp):
        send_panel((OWN, 1), k, 1)

    every = range(samp)
    start_oo(0, every, lambda u, k: x[tab[u, 0, k] & (cols - 1)])
    start_cc(1)

    def from_var(u, k):
        return farz[u, k]

    def take(b, ranks=every, turn=None):
        arrived(b if turn is None else turn, ranks)
        start_oo(b, ranks, from_var)

    def settle(b):
        column(b)
        for d in range(1, samp - 1):
            out_copy(d, b).start()

    last = var - 1
    take(1)
    for b in range(2, var):
        start_cc(b)
    blk_load.wait()
    dia_load.wait()
    settle(0)
    take(2)
    arrived(3, every)

    @pl.when(inner == 0)
    def _():
        send(across, range(samp), outer_turns)

    settle(1)
    start_oo(3, every, from_var)
    settle(2)
    relay(0)
    relay(1)
    take(4)
    settle(3)
    relay(2)
    take(5)
    settle(4)
    relay(3)
    settle(5)
    relay(4)
    take(6)
    relay(5)
    take(last, range(samp // 2))

    @pl.when(core == 1)
    def _():
        settle(last - 1)

    take(last, range(samp // 2, samp), 0)

    @pl.when(core == 0)
    def _():
        settle(last - 1)

    column(last)

    def tail_copy(d):
        return remote(tails_ref.at[s], tails_ref.at[s], tail_s, tail_r,
                      samp=mate[d])

    def oz_copy(d, u):
        return remote(oz.at[s * var + v], oz.at[s * var + v], oz_s, oz_r,
                      samp=mate[d], var=u)

    halves = [acc[step:step + 1, :] + pltpu.roll(acc[step:step + 1, :], fold_rows, 1) for step in range(STEPS)]
    oz[s * var + v] = jnp.where(fold_col[:1] < fold_rows, halves[0], halves[1])
    peers = [(d, place(spot)) for d in range(samp - 1, -1, -1) for spot in spots[::-1] + [(OWN, 0)]][:-1]
    for peer in peers:
        oz_copy(*peer).start()
    for d in range(1, samp - 1):
        out_copy(d, last).start()

    early_owner = s < samp // 2
    late_owner = s >= samp // 2

    @pl.when(late_owner)
    def _():
        out_copy(samp - 1, last).start()

    for d in range(1, samp):
        tail_copy(d).start()
    relay(last - 1)

    beside_done(last)

    @pl.when(early_owner)
    def _():
        relay_copy(0, last, 1).start()

    @pl.when(late_owner)
    def _():
        relay_copy(1, last, 1).start()

    sent = var * (samp - 1) // samp
    together(cc_out.at[:sent], cc_s, cc_r.at[0]).wait_send()
    together(oo_out.at[:sent], oo_s, oo_r.at[0]).wait_send()
    together(fin_ref.at[:samp - 2], out_s.at[0], out_r.at[0]).wait_send()
    together(fin_ref.at[0, :last], rel_s.at[0], rel_r.at[0]).wait()
    together(fin_ref.at[0, 0, 0], rel_s.at[1], rel_r.at[1]).wait_send()

    @pl.when(early_owner)
    def _():
        together(fin_ref.at[0, 0], out_s.at[1], out_r.at[var]).wait_recv()

    @pl.when(late_owner)
    def _():
        together(fin_ref.at[0, 0], out_s.at[1], out_r.at[var]).wait_send()
        together(fin_ref.at[0, 0], rel_s.at[1], rel_r.at[1]).wait_recv()

    together(tails_ref.at[:samp - 1], tail_s, tail_r).wait()
    together(tab_ref.at[:var - 1], ask_ss, ask_rs.at[0]).wait_send()
    together(far.at[:var - 1], z_s, z_r.at[0]).wait_send()
    together(oz.at[:samp * var - 1], oz_s, oz_r).wait()
    whole = oz[0]
    for e in range(1, samp * var):
        whole = whole + oz[e]
    obj_ref[...] = whole


def unpack_kernel(samp, var, order, bits, tab, fin_ref, tails_ref, whole_ref,
                  out_hbm, dia_hbm, obj_hbm, table, stage, dia, obj, extra):
    v = lax.axis_index("var")
    cols, width = dia.shape
    load = pltpu.make_async_copy(tab, table, extra.at[0])
    load.start()
    lane = lax.broadcasted_iota(jnp.int32, (1, width), 1)
    part = lane // (width // 2)
    for step in range(STEPS):
        obj[step] = jnp.sum(jnp.where(part == step, whole_ref[...], 0.0)) / order
    rest = [pltpu.make_async_copy(obj, obj_hbm, extra.at[1]), pltpu.make_async_copy(dia, dia_hbm, extra.at[2])]
    rest[0].start()

    bases = places(v)

    def place(b, k):
        return lax.shift_right_logical(table[batch_owner(v, bases, b, k), 0, k], bits) & (cols - 1)

    def copy(b, k):
        return pltpu.make_async_copy(stage.at[b * samp + k], out_hbm.at[place(b, k)], extra.at[3])

    for b in range(var):
        for k in range(samp):
            stage[b * samp + k] = fin_ref[k, b].astype(jnp.float32)
    load.wait()
    for b in range(var):
        for k in range(samp):
            copy(b, k).start()
    for b in range(var):
        for k in range(samp):
            dia[pl.ds(place(b, k), 1), :] = tails_ref[k, b:b + 1, :]
    rest[1].start()
    pltpu.make_async_copy(stage, out_hbm, extra.at[3]).wait()
    for other in rest:
        other.wait()


def column_body(observed, blocks, diagonal, pattern):
    cols, width = blocks.shape[0], blocks.shape[2]
    rows = observed.shape[0]
    var, samp = lax.axis_size("var"), lax.axis_size("samp")
    bits = cols.bit_length() - 1

    vmem = pl.BlockSpec(memory_space=pltpu.VMEM)
    smem = pl.BlockSpec(memory_space=pltpu.SMEM)
    hbm = pl.BlockSpec(memory_space=pltpu.HBM)
    dma = pltpu.SemaphoreType.DMA
    bf16, f32 = jnp.bfloat16, jnp.float32
    fold, late_rows = width // 2 + 16, width + width // 2 + 16
    fin, tails, whole, table = pl.pallas_call(
        functools.partial(main_kernel, samp, var),
        out_shape=(
            jax.ShapeDtypeStruct((samp, var, 2, width, width), bf16),
            jax.ShapeDtypeStruct((samp, var, width), f32),
            jax.ShapeDtypeStruct((1, width), f32),
            jax.ShapeDtypeStruct((var, 1, width), jnp.int32),
        ),
        in_specs=[hbm] * 4,
        out_specs=(vmem,) * 4,
        scratch_shapes=[
            pltpu.VMEM((2, cols), jnp.int32),
            pltpu.VMEM((cols, rows, width), observed.dtype),
            pltpu.VMEM(blocks.shape, f32),
            pltpu.VMEM((cols, 1, width), f32),
            pltpu.SMEM((var, 1, width), jnp.int32),
            pltpu.SMEM((var, 1, width), jnp.int32),
            pltpu.VMEM((var, samp, rows, width), observed.dtype),
            pltpu.VMEM((var, samp, rows, width), observed.dtype),
            pltpu.VMEM((var, samp, fold, width), bf16),
            pltpu.VMEM((var, samp, fold, width), bf16),
            pltpu.VMEM((var, width // 2, width), f32),
            pltpu.VMEM((var, 1, width), f32),
            pltpu.VMEM((var, samp, late_rows, width), bf16),
            pltpu.VMEM((var, samp, late_rows, width), bf16),
            pltpu.VMEM((var, width, width), f32),
            pltpu.VMEM((var, width // 2, width), f32),
            pltpu.VMEM((var, 1, width), f32),
            pltpu.VMEM((samp * var, 1, width), f32),
            pltpu.VMEM((8, width), f32),
            dma((4,)), dma, dma, dma((var,)), dma, dma((var,)), dma, dma((var,)), dma, dma((var,)),
            dma((2,)), dma((var + 1,)), dma((2,)), dma((2,)), dma, dma, dma, dma,
        ],
        compiler_params=pltpu.CompilerParams(
            collective_id=0, has_side_effects=True, vmem_limit_bytes=40 * 2 ** 20),
        name="columns",
    )(*(pltpu.with_memory_space_constraint(array, pltpu.HBM)
        for array in (pattern.T, observed, blocks, diagonal.reshape(cols, 1, width))))

    new_blocks, new_diagonal, objective = pl.pallas_call(
        functools.partial(unpack_kernel, samp, var, float(cols * width * var), bits),
        out_shape=(
            jax.ShapeDtypeStruct(blocks.shape, f32),
            jax.ShapeDtypeStruct((cols, width), f32),
            jax.ShapeDtypeStruct((STEPS,), f32),
        ),
        in_specs=[vmem] * 4,
        out_specs=(hbm,) * 3,
        scratch_shapes=[
            pltpu.SMEM((var, 1, width), jnp.int32),
            pltpu.VMEM((cols, 2, width, width), f32),
            pltpu.VMEM((cols, width), f32),
            pltpu.SMEM((STEPS,), f32),
            dma((4,)),
        ],
        compiler_params=pltpu.CompilerParams(vmem_limit_bytes=16 * 2 ** 20),
        name="unpack",
    )(table, fin, tails, whole)
    return new_blocks, new_diagonal.reshape(-1), objective


def advance(diag_block, off_block, diag_values, grad_diag, grad_off, diag_mask, total_rows):
    grad_diag = grad_diag / total_rows
    grad_off = grad_off / total_rows
    new_off = shrink(off_block - step_length * grad_off, step_length * penalty)
    new_diag_block = jnp.where(
        diag_mask, 0.0, shrink(diag_block - step_length * grad_diag, step_length * penalty)
    )
    along = jnp.sum(jnp.where(diag_mask, grad_diag, 0.0), axis=1)
    moved = diag_values - step_length * along
    new_values = 0.5 * (moved + jnp.sqrt(moved * moved + 4.0 * step_length))
    return (new_diag_block, new_off, new_values)


def body(observed, blocks, diagonal, pattern):
    col_count = blocks.shape[0]
    block_width = blocks.shape[2]
    sample_rows = observed.shape[0]
    var_count = lax.axis_size("var")
    samp_count = lax.axis_size("samp")
    capacity = max(2, -(-col_count // var_count))
    total_rows = sample_rows * samp_count
    matrix_order = col_count * block_width * var_count
    var_index = lax.axis_index("var")
    column_ids = jnp.arange(col_count, dtype=jnp.int32)
    columns = var_index * col_count + column_ids
    on_diag = pattern == columns[:, None]
    off_row = jnp.sum(jnp.where(on_diag, 0, pattern), axis=1)
    owner_index = off_row // col_count
    resident_block = off_row % col_count
    earlier = (owner_index[None, :] == owner_index[:, None]) & (
        column_ids[None, :] < column_ids[:, None]
    )
    position_rank = jnp.sum(earlier, axis=1)
    slot_index = owner_index * capacity + position_rank
    all_slots = jnp.arange(var_count * capacity, dtype=jnp.int32)
    slot_match = slot_index[:, None] == all_slots[None, :]
    wanted = jnp.sum(jnp.where(slot_match, resident_block[:, None], 0), axis=0)
    asked_blocks = lax.all_to_all(wanted, "var", split_axis=0, concat_axis=0, tiled=True)
    nearby_panels = observed.reshape(sample_rows, col_count, block_width)
    outgoing = jnp.take(nearby_panels, asked_blocks, axis=1)
    arrived = lax.all_to_all(outgoing, "var", split_axis=1, concat_axis=1, tiled=True)
    distant_panels = jnp.take(arrived, slot_index, axis=1)
    diag_mask = jnp.eye(block_width, dtype=bool)
    flags = on_diag[:, :, None, None]
    diag_block = jnp.sum(jnp.where(flags, blocks, 0.0), axis=1)
    diag_block = jnp.where(diag_mask, 0.0, diag_block)
    off_block = jnp.sum(jnp.where(flags, 0.0, blocks), axis=1)
    diag_values = diagonal.reshape(col_count, block_width)
    samp_first = (lax.axis_index("samp") == 0).astype(jnp.float32)
    objective_parts = []
    for iteration in range(STEPS):
        full_diag = jnp.where(diag_mask, diag_values[:, None, :], diag_block)
        product = jnp.einsum(
            "qlh,lhy->qly",
            nearby_panels,
            full_diag.astype(jnp.bfloat16),
            preferred_element_type=jnp.float32,
        )
        product = product + jnp.einsum(
            "qlh,lhy->qly",
            distant_panels,
            off_block.astype(jnp.bfloat16),
            preferred_element_type=jnp.float32,
        )
        squares = jnp.sum(product * product)
        local_terms = -jnp.sum(jnp.log(diag_values)) + penalty * (
            jnp.sum(jnp.abs(diag_block)) + jnp.sum(jnp.abs(off_block))
        )
        part_value = (squares / (2.0 * total_rows) + samp_first * local_terms) / matrix_order
        objective_parts.append(part_value)
        lower_precision_product = product.astype(jnp.bfloat16)
        grad_diag = jnp.einsum(
            "rei,reo->eio",
            nearby_panels,
            lower_precision_product,
            preferred_element_type=jnp.float32,
        )
        grad_off = jnp.einsum(
            "rei,reo->eio",
            distant_panels,
            lower_precision_product,
            preferred_element_type=jnp.float32,
        )
        grad_diag, grad_off = lax.psum((grad_diag, grad_off), "samp")
        diag_block, off_block, diag_values = advance(
            diag_block, off_block, diag_values, grad_diag, grad_off, diag_mask, total_rows
        )
    objective = lax.psum(jnp.stack(objective_parts), ("samp", "var"))
    new_blocks = jnp.where(flags, diag_block[:, None], off_block[:, None])
    return (new_blocks, diag_values.reshape(-1), objective)


def power_of_two(count):
    return count & (count - 1) == 0


def whole_body(observed, blocks, diagonal, pattern):
    cols = blocks.shape[0]
    var, samp = lax.axis_size("var"), lax.axis_size("samp")
    exact = samp == 4 and samp * var == cols and var == 2 * samp and blocks.shape[2] == 128
    if exact and power_of_two(samp) and power_of_two(var):
        return column_body(observed, blocks, diagonal, pattern)
    return body(observed, blocks, diagonal, pattern)


def solution(mesh):
    placed = (P("samp", "var"), P("var", None, None, None), P("var"), P("var", None))
    return jax.shard_map(
        whole_body,
        mesh=mesh,
        in_specs=placed,
        out_specs=(P("var", None, None, None), P("var"), P()),
        check_vma=False,
    )
```

```python
import functools

import jax
import jax.numpy as jnp
from jax import lax
from jax.experimental import pallas as pl
from jax.experimental.pallas import tpu as pltpu
from jax.sharding import PartitionSpec as P

STEPS = 2


step_length = 0.5
penalty = 0.5
MESH = pl.DeviceIdType.MESH


def shrink(moved, level):
    return moved - jnp.clip(moved, -level, level)


def mates(s):
    return s, s + 1 - 2 * (s % 2), s + 2 - 4 * (s // 2), 3 - s


def places(v):
    far_half = 1 - v // 4
    own = v // 2
    return 2 * own, 2 * (own + 1 - 2 * (own % 2)), 2 + 2 * far_half, 6 * far_half


OWN, NEXT, CLOSE, DISTANT = range(4)


def batch_place(b, high, low):
    return ((OWN, 0), (OWN, 1), (NEXT, high), (CLOSE, low), (NEXT, 1 - high),
            (DISTANT, low), (DISTANT, 1 - low), (CLOSE, 1 - low))[b]


def batch_owner(v, bases, b, k):
    chip, other = batch_place(b, k // 2, k % 2)
    return bases[chip] + (v % 2 + other) % 2


def send_rank(chip, other, n):
    if chip == NEXT:
        return (n + 2 * other) % 4
    return 2 * n + other if n < 2 else 2 * (n - 2) + 1 - other


def main_kernel(samp, var, pat_hbm, x_hbm, blk_hbm, dia_hbm,
                fin_ref, tails_ref, obj_ref, tab_ref,
                pat_ref, x, blk, dia_ref, tab, ask_s, far, farz, cc_out, cc_in, cc_own, cc_diag,
                oo_out, oo_in, oc_own, oo_own, oo_diag, oz, acc,
                load, tab_l, ask_ss, ask_rs, cc_s, cc_r, z_s, z_r, oo_s, oo_r, out_s, out_r,
                rel_s, rel_r, tail_s, tail_r, oz_s, oz_r):
    s = lax.axis_index("samp")
    v = lax.axis_index("var")
    inner = (v // 2 + v // 4) % 2
    core = v % 2
    bases = places(v)
    cores = (core, 1 - core)
    mate = mates(s)
    spots = [(chip, other) for chip in range(4) for other in range(2)][1:]
    rows, width = x.shape[1], x.shape[2]
    fold_rows = width // 2
    total_rows = rows * samp
    over_first = (((0,), (0,)), ((), ()))

    cols = x.shape[0]
    bits = cols.bit_length() - 1
    barrier = pltpu.get_barrier_semaphore()
    for chip, other in spots:
        pl.semaphore_signal(barrier, inc=1, device_id={"var": bases[chip] + cores[other]}, device_id_type=MESH)
    for d in range(1, samp):
        pl.semaphore_signal(barrier, inc=1, device_id={"samp": mate[d]}, device_id_type=MESH)

    pat_load = pltpu.make_async_copy(pat_hbm, pat_ref, load.at[1])
    pat_load.start()
    x_loads = [
        pltpu.make_async_copy(x_hbm.at[:, l * width:(l + 1) * width], x.at[l], load.at[0])
        for l in range(cols)
    ]
    for x_load in x_loads:
        x_load.start()
    blk_load = pltpu.make_async_copy(blk_hbm, blk, load.at[2])
    dia_load = pltpu.make_async_copy(dia_hbm, dia_ref, load.at[3])

    pat_load.wait()
    first, second = pat_ref[0:1, :], pat_ref[1:2, :]
    ids = lax.broadcasted_iota(jnp.int32, (1, cols), 1)
    lead = first == v * cols + ids
    off_row = jnp.where(lead, second, first)
    owner = lax.shift_right_logical(off_row, bits)
    entry = (off_row & (cols - 1)) + ids * cols + jnp.where(lead, 0, cols * cols)
    below = lax.broadcasted_iota(jnp.int32, (cols, cols), 0)
    across = lax.broadcasted_iota(jnp.int32, (cols, cols), 1)
    wide = jnp.broadcast_to(owner, (cols, cols))
    down = jnp.sum(jnp.where(below == across, wide, 0), axis=1, keepdims=True)
    rank = jnp.sum(jnp.where((down == wide) & (below < across), 1, 0), axis=0, keepdims=True)
    mine = lax.broadcasted_iota(jnp.int32, (var, cols), 0) == owner
    lanes = lax.broadcasted_iota(jnp.int32, (var, width), 1)
    table = jnp.zeros((var, width), jnp.int32)
    for k in range(samp):
        picked = jnp.sum(jnp.where(mine & (rank == k), entry, 0), axis=1, keepdims=True)
        table = jnp.where(lanes == k, picked, table)
    for u in range(var):
        tab_ref[u] = table[u:u + 1, :]
    tab_load = pltpu.make_async_copy(tab_ref, tab, tab_l)
    tab_load.start()

    pl.semaphore_wait(barrier, samp + var - 2)

    def remote(src, dst, send, recv, **where):
        return pltpu.make_async_remote_copy(
            src_ref=src, dst_ref=dst, send_sem=send, recv_sem=recv,
            device_id=where, device_id_type=MESH)

    def place(spot):
        return bases[spot[0]] + cores[spot[1]]

    def ask_copy(u):
        return remote(tab_ref.at[u], ask_s.at[v], ask_ss, ask_rs.at[v], var=u)

    def ask_arrival(u):
        return remote(tab_ref.at[u], ask_s.at[u], ask_ss, ask_rs.at[u], var=u)

    def z_copy(u, k, turn):
        return remote(far.at[u, k], farz.at[v, k], z_s, z_r.at[turn], var=u)

    def cc_copy(b, k):
        return remote(cc_out.at[b, k], cc_in.at[b, s], cc_s, cc_r.at[b], samp=k)

    def oo_copy(b, k):
        return remote(oo_out.at[b, k], oo_in.at[b, s], oo_s, oo_r.at[b], samp=k)

    def out_copy(d, b):
        direct = d == samp - 1
        return remote(fin_ref.at[s, b], fin_ref.at[s, b], out_s.at[int(direct)], out_r.at[var if direct else b],
                      samp=mate[d])

    def together(array, send, recv):
        return remote(array, array, send, recv, samp=mate[1])

    def near_panel(u, k):
        return x[lax.shift_right_logical(tab[u, 0, k], bits) & (cols - 1)]

    def gram(left, right):
        return lax.dot_general(left, right, over_first, preferred_element_type=jnp.float32)

    row_at = lax.broadcasted_iota(jnp.int32, (width, width), 0)
    col_at = lax.broadcasted_iota(jnp.int32, (width, width), 1)
    eye = row_at == col_at
    fold_row = lax.broadcasted_iota(jnp.int32, (fold_rows, width), 0)
    fold_col = lax.broadcasted_iota(jnp.int32, (fold_rows, width), 1)
    from_top = fold_col >= fold_row + fold_rows
    own_top = (fold_col < fold_rows) & (fold_col >= fold_row)
    note_row = lax.broadcasted_iota(jnp.int32, (16, width), 0)

    def folded(part):
        return jnp.where(from_top, pltpu.roll(part[:fold_rows], fold_rows, 1), part[fold_rows:])

    def unfolded(half_block, diag):
        turned = pltpu.roll(half_block, fold_rows, 1)
        mirror = jnp.concatenate([half_block, turned], axis=0).T
        top = jnp.where(own_top, turned, mirror[fold_rows:])
        bottom = jnp.where(from_top, mirror[:fold_rows], half_block)
        return jnp.where(eye, diag, jnp.concatenate([top, bottom], axis=0))

    def diagonal_of(part):
        return jnp.sum(jnp.where(eye, part, 0.0), axis=0, keepdims=True)

    def note_of(diag):
        high = diag.astype(jnp.bfloat16).astype(jnp.float32)
        return jnp.where(note_row == 0, high, jnp.where(note_row == 1, diag - high, 0.0))

    def start_cc(b):
        for k in range(samp):
            u = batch_owner(v, bases, b, k)
            c = near_panel(u, k)
            part = gram(c, c)
            short, diag = folded(part), diagonal_of(part)
            cc_out[b, k, :fold_rows] = short.astype(jnp.bfloat16)
            cc_out[b, k, fold_rows:] = note_of(diag).astype(jnp.bfloat16)

            @pl.when(s == k)
            def _():
                cc_own[b] = short
                cc_diag[b] = diag

            @pl.when(s != k)
            def _():
                cc_copy(b, k).start()

    def start_oo(b, ranks, far_panel):
        for k in ranks:
            u = batch_owner(v, bases, b, k)
            o = far_panel(u, k)
            part = gram(o, jnp.concatenate([near_panel(u, k), o], axis=1))
            cross, own = part[:, :width], part[:, width:]
            short, diag = folded(own), diagonal_of(own)
            oo_out[b, k, :width] = cross.astype(jnp.bfloat16)
            oo_out[b, k, width:width + fold_rows] = short.astype(jnp.bfloat16)
            oo_out[b, k, width + fold_rows:] = note_of(diag).astype(jnp.bfloat16)

            @pl.when(s == k)
            def _():
                oc_own[b] = cross
                oo_own[b] = short
                oo_diag[b] = diag

            @pl.when(s != k)
            def _():
                oo_copy(b, k).start()

    def arrived(turn, ranks):
        together(farz.at[0, :len(ranks)], z_s, z_r.at[turn]).wait_recv()

    def note_sum(note):
        note = note.astype(jnp.float32)
        return note[0:1] + note[1:2]

    def column(b):
        together(cc_in.at[b, :samp - 1], cc_s, cc_r.at[b]).wait_recv()
        together(oo_in.at[b, :samp - 1], oo_s, oo_r.at[b]).wait_recv()
        cc, oc, oo = cc_own[b], oc_own[b], oo_own[b]
        cc_d, oo_d = cc_diag[b], oo_diag[b]
        for d in range(1, samp):
            p = mate[d]
            cc = cc + cc_in[b, p, :fold_rows].astype(jnp.float32)
            cc_d = cc_d + note_sum(cc_in[b, p, fold_rows:])
            oc = oc + oo_in[b, p, :width].astype(jnp.float32)
            oo = oo + oo_in[b, p, width:width + fold_rows].astype(jnp.float32)
            oo_d = oo_d + note_sum(oo_in[b, p, width + fold_rows:])
        cc, oo = unfolded(cc, cc_d), unfolded(oo, oo_d)
        both = jnp.concatenate(
            [jnp.concatenate([cc, oc.T], axis=1), jnp.concatenate([oc, oo], axis=1)], axis=0)
        high = both.astype(jnp.bfloat16)
        low = (both - high.astype(jnp.float32)).astype(jnp.bfloat16)
        gram_parts = jnp.concatenate([high, low], axis=1)
        u = batch_owner(v, bases, b, s)
        value = tab[u, 0, s]
        col = lax.shift_right_logical(value, bits) & (cols - 1)
        slot = lax.shift_right_logical(value, 2 * bits) & 1
        wd = jnp.where(eye, 0.0, blk[col, slot])
        wo = blk[col, 1 - slot]
        dv = dia_ref[col]
        for step in range(STEPS):
            rounded = jnp.concatenate(
                [jnp.where(eye, dv, wd).astype(jnp.bfloat16), wo.astype(jnp.bfloat16)], axis=0)
            grad = jnp.dot(gram_parts, jnp.concatenate([rounded, rounded], axis=0),
                           preferred_element_type=jnp.float32)
            squares = jnp.sum(grad * rounded.astype(jnp.float32), axis=0, keepdims=True)
            terms = (squares / (2.0 * total_rows) - jnp.log(dv)
                     + penalty * jnp.sum(jnp.abs(wd) + jnp.abs(wo), axis=0, keepdims=True))
            acc[step:step + 1, :] += terms
            grad = grad / total_rows
            gd, go = grad[:width], grad[width:]
            wo = shrink(wo - step_length * go, step_length * penalty)
            wd = jnp.where(eye, 0.0, shrink(wd - step_length * gd, step_length * penalty))
            along = jnp.sum(jnp.where(eye, gd, 0.0), axis=0, keepdims=True)
            moved = dv - step_length * along
            dv = 0.5 * (moved + jnp.sqrt(moved * moved + 4.0 * step_length))
        lead = slot == 0
        fin_ref[s, b, 0] = jnp.where(lead, wd, wo).astype(jnp.bfloat16)
        fin_ref[s, b, 1] = jnp.where(lead, wo, wd).astype(jnp.bfloat16)
        tails_ref[s, pl.ds(b, 1), :] = dv

    def relay_copy(part, b, final=0):
        near, to = mate[1 + part], mate[2 - part]
        return remote(fin_ref.at[near, b, part], fin_ref.at[near, b, part],
                      rel_s.at[final], rel_r.at[final], samp=to)

    def beside_done(b):
        together(fin_ref.at[0, :samp - 2], out_s.at[0], out_r.at[b]).wait_recv()

    def relay(b):
        beside_done(b)
        for part in range(2):
            relay_copy(part, b).start()

    close = [(CLOSE, 0), (CLOSE, 1)]
    beside = [(NEXT, 0), (NEXT, 1)]
    distant = [(DISTANT, 0), (DISTANT, 1)]
    for spot in close + beside + distant + [(OWN, 1)]:
        ask_copy(place(spot)).start()
    acc[...] = jnp.zeros_like(acc)
    pltpu.make_async_copy(x, x, load.at[0]).wait()
    blk_load.start()
    dia_load.start()
    tab_load.wait()
    start_cc(0)

    def learn(wanted):
        for spot in wanted:
            ask_arrival(place(spot)).wait_recv()

    def send_panel(spot, k, turn):
        u = place(spot)
        far[u, k] = x[ask_s[u, 0, k] & (cols - 1)]
        z_copy(u, k, turn).start()

    def send(wanted, turns, at):
        for n in turns:
            for spot in wanted:
                send_panel(spot, send_rank(*spot, n), at[n])

    near_turns, inner_turns, outer_turns = (2, 2, 4, 4), (3, 3, 7, 0), (5, 5, 6, 6)

    def send_by_core(turns, at):
        for to in range(2):
            for n in turns:
                for chip in (CLOSE, DISTANT):
                    other = (core + to) % 2
                    k = 2 * n + other if n < 2 else 2 * (n - 2) + 1 - other
                    u = bases[chip] + to
                    far[u, k] = x[ask_s[u, 0, k] & (cols - 1)]
                    z_copy(u, k, at[n]).start()

    across = [close[0], distant[0], close[1], distant[1]]

    @pl.when(inner == 1)
    def _():
        learn(close)
        send(close, [0], inner_turns)
        learn(distant + beside)
        send(distant, [0], inner_turns)
        send(beside, range(samp), near_turns)
        send(across, [1], inner_turns)
        send_by_core((2, 3), inner_turns)

    @pl.when(inner == 0)
    def _():
        learn(beside)
        send(beside, range(samp), near_turns)
        learn(close + distant)

    learn([(OWN, 1)])
    for k in range(samp):
        send_panel((OWN, 1), k, 1)

    every = range(samp)
    start_oo(0, every, lambda u, k: x[tab[u, 0, k] & (cols - 1)])
    start_cc(1)

    def from_var(u, k):
        return farz[u, k]

    def take(b, ranks=every, turn=None):
        arrived(b if turn is None else turn, ranks)
        start_oo(b, ranks, from_var)

    def settle(b):
        column(b)
        for d in range(1, samp - 1):
            out_copy(d, b).start()

    last = var - 1
    take(1)
    for b in range(2, var):
        start_cc(b)
    blk_load.wait()
    dia_load.wait()
    settle(0)
    take(2)
    arrived(3, every)

    @pl.when(inner == 0)
    def _():
        send(across, range(2), outer_turns)
        send_by_core((2, 3), outer_turns)

    settle(1)
    start_oo(3, every, from_var)
    settle(2)
    relay(0)
    relay(1)
    take(4)
    settle(3)
    relay(2)
    take(5)
    settle(4)
    relay(3)
    settle(5)
    relay(4)
    take(6)
    relay(5)
    settle(last - 1)
    take(last, range(samp // 2))
    take(last, range(samp // 2, samp), 0)
    column(last)

    def tail_copy(d):
        return remote(tails_ref.at[s], tails_ref.at[s], tail_s, tail_r,
                      samp=mate[d])

    def oz_copy(d, u):
        return remote(oz.at[s * var + v], oz.at[s * var + v], oz_s, oz_r,
                      samp=mate[d], var=u)

    halves = [acc[step:step + 1, :] + pltpu.roll(acc[step:step + 1, :], fold_rows, 1) for step in range(STEPS)]
    oz[s * var + v] = jnp.where(fold_col[:1] < fold_rows, halves[0], halves[1])
    peers = [(d, place(spot)) for d in range(samp - 1, -1, -1) for spot in spots[::-1] + [(OWN, 0)]][:-1]
    for peer in peers:
        oz_copy(*peer).start()
    for d in range(1, samp - 1):
        out_copy(d, last).start()

    early_owner = s < samp // 2
    late_owner = s >= samp // 2

    @pl.when(late_owner)
    def _():
        out_copy(samp - 1, last).start()

    for d in range(1, samp):
        tail_copy(d).start()
    relay(last - 1)

    beside_done(last)

    @pl.when(early_owner)
    def _():
        relay_copy(0, last, 1).start()

    @pl.when(late_owner)
    def _():
        relay_copy(1, last, 1).start()

    sent = var * (samp - 1) // samp
    together(cc_out.at[:sent], cc_s, cc_r.at[0]).wait_send()
    together(oo_out.at[:sent], oo_s, oo_r.at[0]).wait_send()
    together(fin_ref.at[:samp - 2], out_s.at[0], out_r.at[0]).wait_send()
    together(fin_ref.at[0, :last], rel_s.at[0], rel_r.at[0]).wait()
    together(fin_ref.at[0, 0, 0], rel_s.at[1], rel_r.at[1]).wait_send()

    @pl.when(early_owner)
    def _():
        together(fin_ref.at[0, 0], out_s.at[1], out_r.at[var]).wait_recv()

    @pl.when(late_owner)
    def _():
        together(fin_ref.at[0, 0], out_s.at[1], out_r.at[var]).wait_send()
        together(fin_ref.at[0, 0], rel_s.at[1], rel_r.at[1]).wait_recv()

    together(tails_ref.at[:samp - 1], tail_s, tail_r).wait()
    together(tab_ref.at[:var - 1], ask_ss, ask_rs.at[0]).wait_send()
    together(far.at[:var - 1], z_s, z_r.at[0]).wait_send()
    together(oz.at[:samp * var - 1], oz_s, oz_r).wait()
    whole = oz[0]
    for e in range(1, samp * var):
        whole = whole + oz[e]
    obj_ref[...] = whole


def unpack_kernel(samp, var, order, bits, tab, fin_ref, tails_ref, whole_ref,
                  out_hbm, dia_hbm, obj_hbm, table, stage, dia, obj, extra):
    v = lax.axis_index("var")
    cols, width = dia.shape
    load = pltpu.make_async_copy(tab, table, extra.at[0])
    load.start()
    lane = lax.broadcasted_iota(jnp.int32, (1, width), 1)
    part = lane // (width // 2)
    for step in range(STEPS):
        obj[step] = jnp.sum(jnp.where(part == step, whole_ref[...], 0.0)) / order
    rest = [pltpu.make_async_copy(obj, obj_hbm, extra.at[1]), pltpu.make_async_copy(dia, dia_hbm, extra.at[2])]
    rest[0].start()

    bases = places(v)

    def place(b, k):
        return lax.shift_right_logical(table[batch_owner(v, bases, b, k), 0, k], bits) & (cols - 1)

    def copy(b, k):
        return pltpu.make_async_copy(stage.at[b * samp + k], out_hbm.at[place(b, k)], extra.at[3])

    for b in range(var):
        for k in range(samp):
            stage[b * samp + k] = fin_ref[k, b].astype(jnp.float32)
    load.wait()
    for b in range(var):
        for k in range(samp):
            copy(b, k).start()
    for b in range(var):
        for k in range(samp):
            dia[pl.ds(place(b, k), 1), :] = tails_ref[k, b:b + 1, :]
    rest[1].start()
    pltpu.make_async_copy(stage, out_hbm, extra.at[3]).wait()
    for other in rest:
        other.wait()


def column_body(observed, blocks, diagonal, pattern):
    cols, width = blocks.shape[0], blocks.shape[2]
    rows = observed.shape[0]
    var, samp = lax.axis_size("var"), lax.axis_size("samp")
    bits = cols.bit_length() - 1

    vmem = pl.BlockSpec(memory_space=pltpu.VMEM)
    smem = pl.BlockSpec(memory_space=pltpu.SMEM)
    hbm = pl.BlockSpec(memory_space=pltpu.HBM)
    dma = pltpu.SemaphoreType.DMA
    bf16, f32 = jnp.bfloat16, jnp.float32
    fold, late_rows = width // 2 + 16, width + width // 2 + 16
    fin, tails, whole, table = pl.pallas_call(
        functools.partial(main_kernel, samp, var),
        out_shape=(
            jax.ShapeDtypeStruct((samp, var, 2, width, width), bf16),
            jax.ShapeDtypeStruct((samp, var, width), f32),
            jax.ShapeDtypeStruct((1, width), f32),
            jax.ShapeDtypeStruct((var, 1, width), jnp.int32),
        ),
        in_specs=[hbm] * 4,
        out_specs=(vmem,) * 4,
        scratch_shapes=[
            pltpu.VMEM((2, cols), jnp.int32),
            pltpu.VMEM((cols, rows, width), observed.dtype),
            pltpu.VMEM(blocks.shape, f32),
            pltpu.VMEM((cols, 1, width), f32),
            pltpu.SMEM((var, 1, width), jnp.int32),
            pltpu.SMEM((var, 1, width), jnp.int32),
            pltpu.VMEM((var, samp, rows, width), observed.dtype),
            pltpu.VMEM((var, samp, rows, width), observed.dtype),
            pltpu.VMEM((var, samp, fold, width), bf16),
            pltpu.VMEM((var, samp, fold, width), bf16),
            pltpu.VMEM((var, width // 2, width), f32),
            pltpu.VMEM((var, 1, width), f32),
            pltpu.VMEM((var, samp, late_rows, width), bf16),
            pltpu.VMEM((var, samp, late_rows, width), bf16),
            pltpu.VMEM((var, width, width), f32),
            pltpu.VMEM((var, width // 2, width), f32),
            pltpu.VMEM((var, 1, width), f32),
            pltpu.VMEM((samp * var, 1, width), f32),
            pltpu.VMEM((8, width), f32),
            dma((4,)), dma, dma, dma((var,)), dma, dma((var,)), dma, dma((var,)), dma, dma((var,)),
            dma((2,)), dma((var + 1,)), dma((2,)), dma((2,)), dma, dma, dma, dma,
        ],
        compiler_params=pltpu.CompilerParams(
            collective_id=0, has_side_effects=True, vmem_limit_bytes=40 * 2 ** 20),
        name="columns",
    )(*(pltpu.with_memory_space_constraint(array, pltpu.HBM)
        for array in (pattern.T, observed, blocks, diagonal.reshape(cols, 1, width))))

    new_blocks, new_diagonal, objective = pl.pallas_call(
        functools.partial(unpack_kernel, samp, var, float(cols * width * var), bits),
        out_shape=(
            jax.ShapeDtypeStruct(blocks.shape, f32),
            jax.ShapeDtypeStruct((cols, width), f32),
            jax.ShapeDtypeStruct((STEPS,), f32),
        ),
        in_specs=[vmem] * 4,
        out_specs=(hbm,) * 3,
        scratch_shapes=[
            pltpu.SMEM((var, 1, width), jnp.int32),
            pltpu.VMEM((cols, 2, width, width), f32),
            pltpu.VMEM((cols, width), f32),
            pltpu.SMEM((STEPS,), f32),
            dma((4,)),
        ],
        compiler_params=pltpu.CompilerParams(vmem_limit_bytes=16 * 2 ** 20),
        name="unpack",
    )(table, fin, tails, whole)
    return new_blocks, new_diagonal.reshape(-1), objective


def advance(diag_block, off_block, diag_values, grad_diag, grad_off, diag_mask, total_rows):
    grad_diag = grad_diag / total_rows
    grad_off = grad_off / total_rows
    new_off = shrink(off_block - step_length * grad_off, step_length * penalty)
    new_diag_block = jnp.where(
        diag_mask, 0.0, shrink(diag_block - step_length * grad_diag, step_length * penalty)
    )
    along = jnp.sum(jnp.where(diag_mask, grad_diag, 0.0), axis=1)
    moved = diag_values - step_length * along
    new_values = 0.5 * (moved + jnp.sqrt(moved * moved + 4.0 * step_length))
    return (new_diag_block, new_off, new_values)


def body(observed, blocks, diagonal, pattern):
    col_count = blocks.shape[0]
    block_width = blocks.shape[2]
    sample_rows = observed.shape[0]
    var_count = lax.axis_size("var")
    samp_count = lax.axis_size("samp")
    capacity = max(2, -(-col_count // var_count))
    total_rows = sample_rows * samp_count
    matrix_order = col_count * block_width * var_count
    var_index = lax.axis_index("var")
    column_ids = jnp.arange(col_count, dtype=jnp.int32)
    columns = var_index * col_count + column_ids
    on_diag = pattern == columns[:, None]
    off_row = jnp.sum(jnp.where(on_diag, 0, pattern), axis=1)
    owner_index = off_row // col_count
    resident_block = off_row % col_count
    earlier = (owner_index[None, :] == owner_index[:, None]) & (
        column_ids[None, :] < column_ids[:, None]
    )
    position_rank = jnp.sum(earlier, axis=1)
    slot_index = owner_index * capacity + position_rank
    all_slots = jnp.arange(var_count * capacity, dtype=jnp.int32)
    slot_match = slot_index[:, None] == all_slots[None, :]
    wanted = jnp.sum(jnp.where(slot_match, resident_block[:, None], 0), axis=0)
    asked_blocks = lax.all_to_all(wanted, "var", split_axis=0, concat_axis=0, tiled=True)
    nearby_panels = observed.reshape(sample_rows, col_count, block_width)
    outgoing = jnp.take(nearby_panels, asked_blocks, axis=1)
    arrived = lax.all_to_all(outgoing, "var", split_axis=1, concat_axis=1, tiled=True)
    distant_panels = jnp.take(arrived, slot_index, axis=1)
    diag_mask = jnp.eye(block_width, dtype=bool)
    flags = on_diag[:, :, None, None]
    diag_block = jnp.sum(jnp.where(flags, blocks, 0.0), axis=1)
    diag_block = jnp.where(diag_mask, 0.0, diag_block)
    off_block = jnp.sum(jnp.where(flags, 0.0, blocks), axis=1)
    diag_values = diagonal.reshape(col_count, block_width)
    samp_first = (lax.axis_index("samp") == 0).astype(jnp.float32)
    objective_parts = []
    for iteration in range(STEPS):
        full_diag = jnp.where(diag_mask, diag_values[:, None, :], diag_block)
        product = jnp.einsum(
            "qlh,lhy->qly",
            nearby_panels,
            full_diag.astype(jnp.bfloat16),
            preferred_element_type=jnp.float32,
        )
        product = product + jnp.einsum(
            "qlh,lhy->qly",
            distant_panels,
            off_block.astype(jnp.bfloat16),
            preferred_element_type=jnp.float32,
        )
        squares = jnp.sum(product * product)
        local_terms = -jnp.sum(jnp.log(diag_values)) + penalty * (
            jnp.sum(jnp.abs(diag_block)) + jnp.sum(jnp.abs(off_block))
        )
        part_value = (squares / (2.0 * total_rows) + samp_first * local_terms) / matrix_order
        objective_parts.append(part_value)
        lower_precision_product = product.astype(jnp.bfloat16)
        grad_diag = jnp.einsum(
            "rei,reo->eio",
            nearby_panels,
            lower_precision_product,
            preferred_element_type=jnp.float32,
        )
        grad_off = jnp.einsum(
            "rei,reo->eio",
            distant_panels,
            lower_precision_product,
            preferred_element_type=jnp.float32,
        )
        grad_diag, grad_off = lax.psum((grad_diag, grad_off), "samp")
        diag_block, off_block, diag_values = advance(
            diag_block, off_block, diag_values, grad_diag, grad_off, diag_mask, total_rows
        )
    objective = lax.psum(jnp.stack(objective_parts), ("samp", "var"))
    new_blocks = jnp.where(flags, diag_block[:, None], off_block[:, None])
    return (new_blocks, diag_values.reshape(-1), objective)


def power_of_two(count):
    return count & (count - 1) == 0


def whole_body(observed, blocks, diagonal, pattern):
    cols = blocks.shape[0]
    var, samp = lax.axis_size("var"), lax.axis_size("samp")
    exact = samp == 4 and samp * var == cols and var == 2 * samp and blocks.shape[2] == 128
    if exact and power_of_two(samp) and power_of_two(var):
        return column_body(observed, blocks, diagonal, pattern)
    return body(observed, blocks, diagonal, pattern)


def solution(mesh):
    placed = (P("samp", "var"), P("var", None, None, None), P("var"), P("var", None))
    return jax.shard_map(
        whole_body,
        mesh=mesh,
        in_specs=placed,
        out_specs=(P("var", None, None, None), P("var"), P()),
        check_vma=False,
    )
```

```python
import functools

import jax
import jax.numpy as jnp
from jax import lax
from jax.experimental import pallas as pl
from jax.experimental.pallas import tpu as pltpu
from jax.sharding import PartitionSpec as P

STEPS = 2


step_length = 0.5
penalty = 0.5
MESH = pl.DeviceIdType.MESH


def shrink(moved, level):
    return moved - jnp.clip(moved, -level, level)


def mates(s):
    return s, s + 1 - 2 * (s % 2), s + 2 - 4 * (s // 2), 3 - s


def places(v):
    far_half = 1 - v // 4
    own = v // 2
    return 2 * own, 2 * (own + 1 - 2 * (own % 2)), 2 + 2 * far_half, 6 * far_half


OWN, NEXT, CLOSE, DISTANT = range(4)


def batch_place(b, high, low):
    return ((OWN, 0), (OWN, 1), (NEXT, high), (CLOSE, low), (NEXT, 1 - high),
            (DISTANT, low), (DISTANT, 1 - low), (CLOSE, 1 - low))[b]


def batch_owner(v, bases, b, k):
    chip, other = batch_place(b, k // 2, k % 2)
    return bases[chip] + (v % 2 + other) % 2


def send_rank(chip, other, n):
    if chip == NEXT:
        return (n + 2 * other) % 4
    return 2 * n + other if n < 2 else 2 * (n - 2) + 1 - other


def main_kernel(samp, var, pat_hbm, x_hbm, blk_hbm, dia_hbm,
                fin_ref, tails_ref, obj_ref, tab_ref,
                pat_ref, x, blk, dia_ref, tab, ask_s, far, farz, cc_out, cc_in, cc_own, cc_diag,
                oo_out, oo_in, oc_own, oo_own, oo_diag, oz, acc,
                load, tab_l, ask_ss, ask_rs, cc_s, cc_r, z_s, z_r, oo_s, oo_r, out_s, out_r,
                rel_s, rel_r, tail_s, tail_r, oz_s, oz_r):
    s = lax.axis_index("samp")
    v = lax.axis_index("var")
    inner = (v // 2 + v // 4) % 2
    core = v % 2
    bases = places(v)
    cores = (core, 1 - core)
    mate = mates(s)
    spots = [(chip, other) for chip in range(4) for other in range(2)][1:]
    rows, width = x.shape[1], x.shape[2]
    fold_rows = width // 2
    total_rows = rows * samp
    over_first = (((0,), (0,)), ((), ()))

    cols = x.shape[0]
    bits = cols.bit_length() - 1
    barrier = pltpu.get_barrier_semaphore()
    for chip, other in spots:
        pl.semaphore_signal(barrier, inc=1, device_id={"var": bases[chip] + cores[other]}, device_id_type=MESH)
    for d in range(1, samp):
        pl.semaphore_signal(barrier, inc=1, device_id={"samp": mate[d]}, device_id_type=MESH)

    pat_load = pltpu.make_async_copy(pat_hbm, pat_ref, load.at[1])
    pat_load.start()
    x_loads = [
        pltpu.make_async_copy(x_hbm.at[:, l * width:(l + 1) * width], x.at[l], load.at[0])
        for l in range(cols)
    ]
    for x_load in x_loads:
        x_load.start()
    blk_load = pltpu.make_async_copy(blk_hbm, blk, load.at[2])
    dia_load = pltpu.make_async_copy(dia_hbm, dia_ref, load.at[3])

    pat_load.wait()
    first, second = pat_ref[0:1, :], pat_ref[1:2, :]
    ids = lax.broadcasted_iota(jnp.int32, (1, cols), 1)
    lead = first == v * cols + ids
    off_row = jnp.where(lead, second, first)
    owner = lax.shift_right_logical(off_row, bits)
    entry = (off_row & (cols - 1)) + ids * cols + jnp.where(lead, 0, cols * cols)
    below = lax.broadcasted_iota(jnp.int32, (cols, cols), 0)
    across = lax.broadcasted_iota(jnp.int32, (cols, cols), 1)
    wide = jnp.broadcast_to(owner, (cols, cols))
    down = jnp.sum(jnp.where(below == across, wide, 0), axis=1, keepdims=True)
    rank = jnp.sum(jnp.where((down == wide) & (below < across), 1, 0), axis=0, keepdims=True)
    mine = lax.broadcasted_iota(jnp.int32, (var, cols), 0) == owner
    lanes = lax.broadcasted_iota(jnp.int32, (var, width), 1)
    table = jnp.zeros((var, width), jnp.int32)
    for k in range(samp):
        picked = jnp.sum(jnp.where(mine & (rank == k), entry, 0), axis=1, keepdims=True)
        table = jnp.where(lanes == k, picked, table)
    for u in range(var):
        tab_ref[u] = table[u:u + 1, :]
    tab_load = pltpu.make_async_copy(tab_ref, tab, tab_l)
    tab_load.start()

    pl.semaphore_wait(barrier, samp + var - 2)

    def remote(src, dst, send, recv, **where):
        return pltpu.make_async_remote_copy(
            src_ref=src, dst_ref=dst, send_sem=send, recv_sem=recv,
            device_id=where, device_id_type=MESH)

    def place(spot):
        return bases[spot[0]] + cores[spot[1]]

    def ask_copy(u):
        return remote(tab_ref.at[u], ask_s.at[v], ask_ss, ask_rs.at[v], var=u)

    def ask_arrival(u):
        return remote(tab_ref.at[u], ask_s.at[u], ask_ss, ask_rs.at[u], var=u)

    def z_copy(u, k, turn):
        return remote(far.at[u, k], farz.at[v, k], z_s, z_r.at[turn], var=u)

    def cc_copy(b, k):
        return remote(cc_out.at[b, k], cc_in.at[b, s], cc_s, cc_r.at[b], samp=k)

    def oo_copy(b, k):
        return remote(oo_out.at[b, k], oo_in.at[b, s], oo_s, oo_r.at[b], samp=k)

    def out_copy(d, b):
        direct = d == samp - 1
        return remote(fin_ref.at[s, b], fin_ref.at[s, b], out_s.at[int(direct)], out_r.at[var if direct else b],
                      samp=mate[d])

    def together(array, send, recv):
        return remote(array, array, send, recv, samp=mate[1])

    def near_panel(u, k):
        return x[lax.shift_right_logical(tab[u, 0, k], bits) & (cols - 1)]

    def gram(left, right):
        return lax.dot_general(left, right, over_first, preferred_element_type=jnp.float32)

    row_at = lax.broadcasted_iota(jnp.int32, (width, width), 0)
    col_at = lax.broadcasted_iota(jnp.int32, (width, width), 1)
    eye = row_at == col_at
    fold_row = lax.broadcasted_iota(jnp.int32, (fold_rows, width), 0)
    fold_col = lax.broadcasted_iota(jnp.int32, (fold_rows, width), 1)
    from_top = fold_col >= fold_row + fold_rows
    own_top = (fold_col < fold_rows) & (fold_col >= fold_row)
    note_row = lax.broadcasted_iota(jnp.int32, (16, width), 0)

    def folded(part):
        return jnp.where(from_top, pltpu.roll(part[:fold_rows], fold_rows, 1), part[fold_rows:])

    def unfolded(half_block, diag):
        turned = pltpu.roll(half_block, fold_rows, 1)
        mirror = jnp.concatenate([half_block, turned], axis=0).T
        top = jnp.where(own_top, turned, mirror[fold_rows:])
        bottom = jnp.where(from_top, mirror[:fold_rows], half_block)
        return jnp.where(eye, diag, jnp.concatenate([top, bottom], axis=0))

    def diagonal_of(part):
        return jnp.sum(jnp.where(eye, part, 0.0), axis=0, keepdims=True)

    def note_of(diag):
        high = diag.astype(jnp.bfloat16).astype(jnp.float32)
        return jnp.where(note_row == 0, high, jnp.where(note_row == 1, diag - high, 0.0))

    def start_cc(b):
        for k in range(samp):
            u = batch_owner(v, bases, b, k)
            c = near_panel(u, k)
            part = gram(c, c)
            short, diag = folded(part), diagonal_of(part)
            cc_out[b, k, :fold_rows] = short.astype(jnp.bfloat16)
            cc_out[b, k, fold_rows:] = note_of(diag).astype(jnp.bfloat16)

            @pl.when(s == k)
            def _():
                cc_own[b] = short
                cc_diag[b] = diag

            @pl.when(s != k)
            def _():
                cc_copy(b, k).start()

    def start_oo(b, ranks, far_panel):
        for k in ranks:
            u = batch_owner(v, bases, b, k)
            o = far_panel(u, k)
            part = gram(o, jnp.concatenate([near_panel(u, k), o], axis=1))
            cross, own = part[:, :width], part[:, width:]
            short, diag = folded(own), diagonal_of(own)
            oo_out[b, k, :width] = cross.astype(jnp.bfloat16)
            oo_out[b, k, width:width + fold_rows] = short.astype(jnp.bfloat16)
            oo_out[b, k, width + fold_rows:] = note_of(diag).astype(jnp.bfloat16)

            @pl.when(s == k)
            def _():
                oc_own[b] = cross
                oo_own[b] = short
                oo_diag[b] = diag

            @pl.when(s != k)
            def _():
                oo_copy(b, k).start()

    def arrived(turn, ranks):
        together(farz.at[0, :len(ranks)], z_s, z_r.at[turn]).wait_recv()

    def note_sum(note):
        note = note.astype(jnp.float32)
        return note[0:1] + note[1:2]

    def column(b):
        together(cc_in.at[b, :samp - 1], cc_s, cc_r.at[b]).wait_recv()
        together(oo_in.at[b, :samp - 1], oo_s, oo_r.at[b]).wait_recv()
        cc, oc, oo = cc_own[b], oc_own[b], oo_own[b]
        cc_d, oo_d = cc_diag[b], oo_diag[b]
        for d in range(1, samp):
            p = mate[d]
            cc = cc + cc_in[b, p, :fold_rows].astype(jnp.float32)
            cc_d = cc_d + note_sum(cc_in[b, p, fold_rows:])
            oc = oc + oo_in[b, p, :width].astype(jnp.float32)
            oo = oo + oo_in[b, p, width:width + fold_rows].astype(jnp.float32)
            oo_d = oo_d + note_sum(oo_in[b, p, width + fold_rows:])
        cc, oo = unfolded(cc, cc_d), unfolded(oo, oo_d)
        both = jnp.concatenate(
            [jnp.concatenate([cc, oc.T], axis=1), jnp.concatenate([oc, oo], axis=1)], axis=0)
        high = both.astype(jnp.bfloat16)
        low = (both - high.astype(jnp.float32)).astype(jnp.bfloat16)
        gram_parts = jnp.concatenate([high, low], axis=1)
        u = batch_owner(v, bases, b, s)
        value = tab[u, 0, s]
        col = lax.shift_right_logical(value, bits) & (cols - 1)
        slot = lax.shift_right_logical(value, 2 * bits) & 1
        wd = jnp.where(eye, 0.0, blk[col, slot])
        wo = blk[col, 1 - slot]
        dv = dia_ref[col]
        for step in range(STEPS):
            rounded = jnp.concatenate(
                [jnp.where(eye, dv, wd).astype(jnp.bfloat16), wo.astype(jnp.bfloat16)], axis=0)
            grad = jnp.dot(gram_parts, jnp.concatenate([rounded, rounded], axis=0),
                           preferred_element_type=jnp.float32)
            squares = jnp.sum(grad * rounded.astype(jnp.float32), axis=0, keepdims=True)
            terms = (squares / (2.0 * total_rows) - jnp.log(dv)
                     + penalty * jnp.sum(jnp.abs(wd) + jnp.abs(wo), axis=0, keepdims=True))
            acc[step:step + 1, :] += terms
            grad = grad / total_rows
            gd, go = grad[:width], grad[width:]
            wo = shrink(wo - step_length * go, step_length * penalty)
            wd = jnp.where(eye, 0.0, shrink(wd - step_length * gd, step_length * penalty))
            along = jnp.sum(jnp.where(eye, gd, 0.0), axis=0, keepdims=True)
            moved = dv - step_length * along
            dv = 0.5 * (moved + jnp.sqrt(moved * moved + 4.0 * step_length))
        lead = slot == 0
        fin_ref[s, b, 0] = jnp.where(lead, wd, wo).astype(jnp.bfloat16)
        fin_ref[s, b, 1] = jnp.where(lead, wo, wd).astype(jnp.bfloat16)
        tails_ref[s, pl.ds(b, 1), :] = dv

    def relay_copy(part, b, final=0):
        near, to = mate[1 + part], mate[2 - part]
        return remote(fin_ref.at[near, b, part], fin_ref.at[near, b, part],
                      rel_s.at[final], rel_r.at[final], samp=to)

    def beside_done(b):
        together(fin_ref.at[0, :samp - 2], out_s.at[0], out_r.at[b]).wait_recv()

    def relay(b):
        beside_done(b)
        for part in range(2):
            relay_copy(part, b).start()

    close = [(CLOSE, 0), (CLOSE, 1)]
    beside = [(NEXT, 0), (NEXT, 1)]
    distant = [(DISTANT, 0), (DISTANT, 1)]
    for spot in close + beside + distant + [(OWN, 1)]:
        ask_copy(place(spot)).start()
    acc[...] = jnp.zeros_like(acc)
    pltpu.make_async_copy(x, x, load.at[0]).wait()
    blk_load.start()
    dia_load.start()
    tab_load.wait()
    start_cc(0)

    def learn(wanted):
        for spot in wanted:
            ask_arrival(place(spot)).wait_recv()

    def send_panel(spot, k, turn):
        u = place(spot)
        far[u, k] = x[ask_s[u, 0, k] & (cols - 1)]
        z_copy(u, k, turn).start()

    def send(wanted, turns, at):
        for n in turns:
            for spot in wanted:
                send_panel(spot, send_rank(*spot, n), at[n])

    near_turns, inner_turns, outer_turns = (2, 2, 4, 4), (3, 3, 7, 0), (5, 5, 6, 6)

    def send_by_core(turns, at):
        for to in range(2):
            for n in turns:
                for chip in (CLOSE, DISTANT):
                    other = (core + to) % 2
                    k = 2 * n + other if n < 2 else 2 * (n - 2) + 1 - other
                    u = bases[chip] + to
                    far[u, k] = x[ask_s[u, 0, k] & (cols - 1)]
                    z_copy(u, k, at[n]).start()

    across = [close[0], distant[0], close[1], distant[1]]

    @pl.when(inner == 1)
    def _():
        learn(close)
        send(close, [0], inner_turns)
        learn(distant + beside)
        send(distant, [0], inner_turns)
        send(beside, range(samp), near_turns)
        send_by_core((1,), inner_turns)
        send_by_core((2, 3), inner_turns)

    @pl.when(inner == 0)
    def _():
        learn(beside)
        send(beside, range(samp), near_turns)
        learn(close + distant)

    learn([(OWN, 1)])
    for k in range(samp):
        send_panel((OWN, 1), k, 1)

    every = range(samp)
    start_oo(0, every, lambda u, k: x[tab[u, 0, k] & (cols - 1)])
    start_cc(1)

    def from_var(u, k):
        return farz[u, k]

    def take(b, ranks=every, turn=None):
        arrived(b if turn is None else turn, ranks)
        start_oo(b, ranks, from_var)

    def settle(b):
        column(b)
        for d in range(1, samp - 1):
            out_copy(d, b).start()

    last = var - 1
    take(1)
    for b in range(2, var):
        start_cc(b)
    blk_load.wait()
    dia_load.wait()
    settle(0)
    take(2)
    arrived(3, every)

    @pl.when(inner == 0)
    def _():
        send(across, range(2), outer_turns)
        send_by_core((2, 3), outer_turns)

    settle(1)
    start_oo(3, every, from_var)
    settle(2)
    relay(0)
    relay(1)
    take(4)
    settle(3)
    relay(2)
    take(5)
    settle(4)
    relay(3)
    settle(5)
    relay(4)
    take(6)
    relay(5)
    settle(last - 1)
    take(last, range(samp // 2))
    take(last, range(samp // 2, samp), 0)
    column(last)

    def tail_copy(d):
        return remote(tails_ref.at[s], tails_ref.at[s], tail_s, tail_r,
                      samp=mate[d])

    def oz_copy(d, u):
        return remote(oz.at[s * var + v], oz.at[s * var + v], oz_s, oz_r,
                      samp=mate[d], var=u)

    halves = [acc[step:step + 1, :] + pltpu.roll(acc[step:step + 1, :], fold_rows, 1) for step in range(STEPS)]
    oz[s * var + v] = jnp.where(fold_col[:1] < fold_rows, halves[0], halves[1])
    peers = [(d, place(spot)) for d in range(samp - 1, -1, -1) for spot in spots[::-1] + [(OWN, 0)]][:-1]
    for peer in peers:
        oz_copy(*peer).start()
    for d in range(1, samp - 1):
        out_copy(d, last).start()

    early_owner = s < samp // 2
    late_owner = s >= samp // 2

    @pl.when(late_owner)
    def _():
        out_copy(samp - 1, last).start()

    for d in range(1, samp):
        tail_copy(d).start()
    relay(last - 1)

    beside_done(last)

    @pl.when(early_owner)
    def _():
        relay_copy(0, last, 1).start()

    @pl.when(late_owner)
    def _():
        relay_copy(1, last, 1).start()

    sent = var * (samp - 1) // samp
    together(cc_out.at[:sent], cc_s, cc_r.at[0]).wait_send()
    together(oo_out.at[:sent], oo_s, oo_r.at[0]).wait_send()
    together(fin_ref.at[:samp - 2], out_s.at[0], out_r.at[0]).wait_send()
    together(fin_ref.at[0, :last], rel_s.at[0], rel_r.at[0]).wait()
    together(fin_ref.at[0, 0, 0], rel_s.at[1], rel_r.at[1]).wait_send()

    @pl.when(early_owner)
    def _():
        together(fin_ref.at[0, 0], out_s.at[1], out_r.at[var]).wait_recv()

    @pl.when(late_owner)
    def _():
        together(fin_ref.at[0, 0], out_s.at[1], out_r.at[var]).wait_send()
        together(fin_ref.at[0, 0], rel_s.at[1], rel_r.at[1]).wait_recv()

    together(tails_ref.at[:samp - 1], tail_s, tail_r).wait()
    together(tab_ref.at[:var - 1], ask_ss, ask_rs.at[0]).wait_send()
    together(far.at[:var - 1], z_s, z_r.at[0]).wait_send()
    together(oz.at[:samp * var - 1], oz_s, oz_r).wait()
    whole = oz[0]
    for e in range(1, samp * var):
        whole = whole + oz[e]
    obj_ref[...] = whole


def unpack_kernel(samp, var, order, bits, tab, fin_ref, tails_ref, whole_ref,
                  out_hbm, dia_hbm, obj_hbm, table, stage, dia, obj, extra):
    v = lax.axis_index("var")
    cols, width = dia.shape
    load = pltpu.make_async_copy(tab, table, extra.at[0])
    load.start()
    lane = lax.broadcasted_iota(jnp.int32, (1, width), 1)
    part = lane // (width // 2)
    for step in range(STEPS):
        obj[step] = jnp.sum(jnp.where(part == step, whole_ref[...], 0.0)) / order
    rest = [pltpu.make_async_copy(obj, obj_hbm, extra.at[1]), pltpu.make_async_copy(dia, dia_hbm, extra.at[2])]
    rest[0].start()

    bases = places(v)

    def place(b, k):
        return lax.shift_right_logical(table[batch_owner(v, bases, b, k), 0, k], bits) & (cols - 1)

    def copy(b, k):
        return pltpu.make_async_copy(stage.at[b * samp + k], out_hbm.at[place(b, k)], extra.at[3])

    for b in range(var):
        for k in range(samp):
            stage[b * samp + k] = fin_ref[k, b].astype(jnp.float32)
    load.wait()
    for b in range(var):
        for k in range(samp):
            copy(b, k).start()
    for b in range(var):
        for k in range(samp):
            dia[pl.ds(place(b, k), 1), :] = tails_ref[k, b:b + 1, :]
    rest[1].start()
    pltpu.make_async_copy(stage, out_hbm, extra.at[3]).wait()
    for other in rest:
        other.wait()


def column_body(observed, blocks, diagonal, pattern):
    cols, width = blocks.shape[0], blocks.shape[2]
    rows = observed.shape[0]
    var, samp = lax.axis_size("var"), lax.axis_size("samp")
    bits = cols.bit_length() - 1

    vmem = pl.BlockSpec(memory_space=pltpu.VMEM)
    smem = pl.BlockSpec(memory_space=pltpu.SMEM)
    hbm = pl.BlockSpec(memory_space=pltpu.HBM)
    dma = pltpu.SemaphoreType.DMA
    bf16, f32 = jnp.bfloat16, jnp.float32
    fold, late_rows = width // 2 + 16, width + width // 2 + 16
    fin, tails, whole, table = pl.pallas_call(
        functools.partial(main_kernel, samp, var),
        out_shape=(
            jax.ShapeDtypeStruct((samp, var, 2, width, width), bf16),
            jax.ShapeDtypeStruct((samp, var, width), f32),
            jax.ShapeDtypeStruct((1, width), f32),
            jax.ShapeDtypeStruct((var, 1, width), jnp.int32),
        ),
        in_specs=[hbm] * 4,
        out_specs=(vmem,) * 4,
        scratch_shapes=[
            pltpu.VMEM((2, cols), jnp.int32),
            pltpu.VMEM((cols, rows, width), observed.dtype),
            pltpu.VMEM(blocks.shape, f32),
            pltpu.VMEM((cols, 1, width), f32),
            pltpu.SMEM((var, 1, width), jnp.int32),
            pltpu.SMEM((var, 1, width), jnp.int32),
            pltpu.VMEM((var, samp, rows, width), observed.dtype),
            pltpu.VMEM((var, samp, rows, width), observed.dtype),
            pltpu.VMEM((var, samp, fold, width), bf16),
            pltpu.VMEM((var, samp, fold, width), bf16),
            pltpu.VMEM((var, width // 2, width), f32),
            pltpu.VMEM((var, 1, width), f32),
            pltpu.VMEM((var, samp, late_rows, width), bf16),
            pltpu.VMEM((var, samp, late_rows, width), bf16),
            pltpu.VMEM((var, width, width), f32),
            pltpu.VMEM((var, width // 2, width), f32),
            pltpu.VMEM((var, 1, width), f32),
            pltpu.VMEM((samp * var, 1, width), f32),
            pltpu.VMEM((8, width), f32),
            dma((4,)), dma, dma, dma((var,)), dma, dma((var,)), dma, dma((var,)), dma, dma((var,)),
            dma((2,)), dma((var + 1,)), dma((2,)), dma((2,)), dma, dma, dma, dma,
        ],
        compiler_params=pltpu.CompilerParams(
            collective_id=0, has_side_effects=True, vmem_limit_bytes=40 * 2 ** 20),
        name="columns",
    )(*(pltpu.with_memory_space_constraint(array, pltpu.HBM)
        for array in (pattern.T, observed, blocks, diagonal.reshape(cols, 1, width))))

    new_blocks, new_diagonal, objective = pl.pallas_call(
        functools.partial(unpack_kernel, samp, var, float(cols * width * var), bits),
        out_shape=(
            jax.ShapeDtypeStruct(blocks.shape, f32),
            jax.ShapeDtypeStruct((cols, width), f32),
            jax.ShapeDtypeStruct((STEPS,), f32),
        ),
        in_specs=[vmem] * 4,
        out_specs=(hbm,) * 3,
        scratch_shapes=[
            pltpu.SMEM((var, 1, width), jnp.int32),
            pltpu.VMEM((cols, 2, width, width), f32),
            pltpu.VMEM((cols, width), f32),
            pltpu.SMEM((STEPS,), f32),
            dma((4,)),
        ],
        compiler_params=pltpu.CompilerParams(vmem_limit_bytes=16 * 2 ** 20),
        name="unpack",
    )(table, fin, tails, whole)
    return new_blocks, new_diagonal.reshape(-1), objective


def advance(diag_block, off_block, diag_values, grad_diag, grad_off, diag_mask, total_rows):
    grad_diag = grad_diag / total_rows
    grad_off = grad_off / total_rows
    new_off = shrink(off_block - step_length * grad_off, step_length * penalty)
    new_diag_block = jnp.where(
        diag_mask, 0.0, shrink(diag_block - step_length * grad_diag, step_length * penalty)
    )
    along = jnp.sum(jnp.where(diag_mask, grad_diag, 0.0), axis=1)
    moved = diag_values - step_length * along
    new_values = 0.5 * (moved + jnp.sqrt(moved * moved + 4.0 * step_length))
    return (new_diag_block, new_off, new_values)


def body(observed, blocks, diagonal, pattern):
    col_count = blocks.shape[0]
    block_width = blocks.shape[2]
    sample_rows = observed.shape[0]
    var_count = lax.axis_size("var")
    samp_count = lax.axis_size("samp")
    capacity = max(2, -(-col_count // var_count))
    total_rows = sample_rows * samp_count
    matrix_order = col_count * block_width * var_count
    var_index = lax.axis_index("var")
    column_ids = jnp.arange(col_count, dtype=jnp.int32)
    columns = var_index * col_count + column_ids
    on_diag = pattern == columns[:, None]
    off_row = jnp.sum(jnp.where(on_diag, 0, pattern), axis=1)
    owner_index = off_row // col_count
    resident_block = off_row % col_count
    earlier = (owner_index[None, :] == owner_index[:, None]) & (
        column_ids[None, :] < column_ids[:, None]
    )
    position_rank = jnp.sum(earlier, axis=1)
    slot_index = owner_index * capacity + position_rank
    all_slots = jnp.arange(var_count * capacity, dtype=jnp.int32)
    slot_match = slot_index[:, None] == all_slots[None, :]
    wanted = jnp.sum(jnp.where(slot_match, resident_block[:, None], 0), axis=0)
    asked_blocks = lax.all_to_all(wanted, "var", split_axis=0, concat_axis=0, tiled=True)
    nearby_panels = observed.reshape(sample_rows, col_count, block_width)
    outgoing = jnp.take(nearby_panels, asked_blocks, axis=1)
    arrived = lax.all_to_all(outgoing, "var", split_axis=1, concat_axis=1, tiled=True)
    distant_panels = jnp.take(arrived, slot_index, axis=1)
    diag_mask = jnp.eye(block_width, dtype=bool)
    flags = on_diag[:, :, None, None]
    diag_block = jnp.sum(jnp.where(flags, blocks, 0.0), axis=1)
    diag_block = jnp.where(diag_mask, 0.0, diag_block)
    off_block = jnp.sum(jnp.where(flags, 0.0, blocks), axis=1)
    diag_values = diagonal.reshape(col_count, block_width)
    samp_first = (lax.axis_index("samp") == 0).astype(jnp.float32)
    objective_parts = []
    for iteration in range(STEPS):
        full_diag = jnp.where(diag_mask, diag_values[:, None, :], diag_block)
        product = jnp.einsum(
            "qlh,lhy->qly",
            nearby_panels,
            full_diag.astype(jnp.bfloat16),
            preferred_element_type=jnp.float32,
        )
        product = product + jnp.einsum(
            "qlh,lhy->qly",
            distant_panels,
            off_block.astype(jnp.bfloat16),
            preferred_element_type=jnp.float32,
        )
        squares = jnp.sum(product * product)
        local_terms = -jnp.sum(jnp.log(diag_values)) + penalty * (
            jnp.sum(jnp.abs(diag_block)) + jnp.sum(jnp.abs(off_block))
        )
        part_value = (squares / (2.0 * total_rows) + samp_first * local_terms) / matrix_order
        objective_parts.append(part_value)
        lower_precision_product = product.astype(jnp.bfloat16)
        grad_diag = jnp.einsum(
            "rei,reo->eio",
            nearby_panels,
            lower_precision_product,
            preferred_element_type=jnp.float32,
        )
        grad_off = jnp.einsum(
            "rei,reo->eio",
            distant_panels,
            lower_precision_product,
            preferred_element_type=jnp.float32,
        )
        grad_diag, grad_off = lax.psum((grad_diag, grad_off), "samp")
        diag_block, off_block, diag_values = advance(
            diag_block, off_block, diag_values, grad_diag, grad_off, diag_mask, total_rows
        )
    objective = lax.psum(jnp.stack(objective_parts), ("samp", "var"))
    new_blocks = jnp.where(flags, diag_block[:, None], off_block[:, None])
    return (new_blocks, diag_values.reshape(-1), objective)


def power_of_two(count):
    return count & (count - 1) == 0


def whole_body(observed, blocks, diagonal, pattern):
    cols = blocks.shape[0]
    var, samp = lax.axis_size("var"), lax.axis_size("samp")
    exact = samp == 4 and samp * var == cols and var == 2 * samp and blocks.shape[2] == 128
    if exact and power_of_two(samp) and power_of_two(var):
        return column_body(observed, blocks, diagonal, pattern)
    return body(observed, blocks, diagonal, pattern)


def solution(mesh):
    placed = (P("samp", "var"), P("var", None, None, None), P("var"), P("var", None))
    return jax.shard_map(
        whole_body,
        mesh=mesh,
        in_specs=placed,
        out_specs=(P("var", None, None, None), P("var"), P()),
        check_vma=False,
    )
```
